256 devices in a mesh: lon: 32 (over x, z_lo, core), lat: 8 (over y, z_hi).
Axes of the slice: x: 4, y: 4, z: 8 (z_hi: 2, z_lo: 4; z = z_hi * 4 + z_lo), core: 2. Of those that a mesh axis runs over, the one named last changes fastest.
Arguments:
- state: float32 [3, 256, 64, 8192], P(None, None, 'lat', 'lon'), may hold values from -6 to 6
- bathymetry: float32 [64, 8192], P('lat', 'lon'), may hold values from 0.5 to 2
- obs_index: int32 [8, 32, 256], P('lat', 'lon'), may hold values from 0 to 2047
- obs_count: int32 [8, 32], P('lat', 'lon'), may hold values from 85 to 256, as said below
- obs_value: float32 [8, 32, 256], P('lat', 'lon'), may hold values from -6 to 6
- obs_sd: float32 [8, 32, 256], P('lat', 'lon'), may hold values from 0.5 to 2
Outputs:
- analysis: float32 [3, 256, 64, 8192], P(None, None, 'lat', 'lon')
The draws below stay inside these ranges and needn't reach their ends.
Inputs may be any that keep to these rules, and one draw needn't show every extreme that they name: `obs_count`: at least 85 slots of every tile are used; at least one tile uses all 256. `obs_index`: several slots may name the same cell.
All inputs are finite; a program needn't handle non-finite values.
Results may differ from the reference program's by a relative error of at most 0.000051.
Values sent between devices are 32-bit elements; how exact they have to be, the bound alone decides.
No kernel may reach another device: no remote copies, remote signals or barrier semaphores. Data moves between devices by JAX's collectives and lax.ppermute only.
A program may use at most 128 MiB of HBM per device.

```python
import math
import jax
import jax.numpy as jnp
from jax import lax

M = 256
CLAT = 8
CLON = 256
KOBS = 256
TLAT = 8
TLON = 32
NLAT = 64
NLON = 8192
NOBS = 65536


def draw_obs_count(key, part):
    first, second = jax.random.split(jax.random.fold_in(key, 17))
    counts = jax.random.randint(first, (TLAT * TLON,), KOBS // 3, KOBS + 1)
    spot = jax.random.randint(second, (), 0, TLAT * TLON)
    counts = jnp.where(jnp.arange(TLAT * TLON) == spot, KOBS, counts)
    return counts.reshape(TLAT, TLON).astype(jnp.int32)


def place_ends(array, rng, least, high):
    longest = array.shape.index(max(array.shape))
    spots = []
    for shift in (0, 1):
        where = [jax.random.randint(jax.random.fold_in(rng, axis), (), 0, length) for axis, length in enumerate(array.shape)]
        where[longest] = (where[longest] + shift) % array.shape[longest]
        spots.append(tuple(where))
    return array.at[spots[0]].set(least).at[spots[1]].set(high)


def level_of(key, extent, cuts, smallest, top_value):
    loudness, own = 1.0, jax.random.fold_in(key, 6)
    for dim, shards_of in cuts:
        steps = jnp.exp(jax.random.uniform(jax.random.fold_in(own, dim), (shards_of,), jnp.float32, smallest / len(cuts), top_value / len(cuts)))
        loudness = loudness * jnp.repeat(steps, extent[dim] // shards_of).reshape([-1 if axis == dim else 1 for axis in range(len(extent))])
    return loudness


def noise(rng, shape, spread, bound, cuts=(), kind=jnp.bfloat16):
    values = spread * jax.random.normal(rng, shape, jnp.float32)
    if cuts:
        values = values * level_of(rng, shape, cuts, -0.22, 0.18)
    return jnp.clip(values, -bound, bound).astype(kind)


def setup_inputs(seed: int = 0) -> dict:
    arg_keys = jax.random.split(jax.random.key(seed), 7)
    return {
        "state": noise(arg_keys[0], (3, M, NLAT, NLON), 1.0, 6.0, ((2, 8), (3, 32)), jnp.float32),
        "bathymetry": jnp.clip(jnp.exp(math.log(2.0) - 1.3862944 * jax.random.uniform(arg_keys[1], (NLAT, NLON), jnp.float32) ** level_of(arg_keys[1], (NLAT, NLON), ((0, 8), (1, 32)), -0.2, 0.2)), 0.5, 2.0),
        "obs_index": place_ends(jax.random.randint(arg_keys[2], (TLAT, TLON, KOBS), 0, CLAT * CLON), jax.random.fold_in(arg_keys[2], 1), 0, (CLAT * CLON) - 1).astype(jnp.int32),
        "obs_count": draw_obs_count(jax.random.fold_in(arg_keys[6], 71), 0),
        "obs_value": noise(arg_keys[4], (TLAT, TLON, KOBS), 1.0, 6.0, ((0, 8), (1, 32)), jnp.float32),
        "obs_sd": jnp.clip(jnp.exp(math.log(2.0) - 1.3862944 * jax.random.uniform(arg_keys[5], (TLAT, TLON, KOBS), jnp.float32) ** level_of(arg_keys[5], (TLAT, TLON, KOBS), ((0, 8), (1, 32)), -0.2, 0.2)), 0.5, 2.0),
    }


def pad_rim(field):
    wrapped = jnp.concatenate([field[..., -1:], field, field[..., :1]], axis=-1)
    widths = [(0, 0)] * (field.ndim - 2) + [(1, 1), (0, 0)]
    return jnp.pad(wrapped, widths)

def reference(state, bathymetry, obs_index, obs_count, obs_value, obs_sd):
    rows = jnp.arange(NLAT).astype(jnp.float32)
    fcor = jnp.sin(math.pi / 3.0 * ((rows + 0.5) / NLAT - 0.5))[:, None]
    height, east, north = (state[0], state[1], state[2])
    for step in range(2):
        flux_x = pad_rim(bathymetry * east)
        flux_y = pad_rim(bathymetry * north)
        div = flux_x[:, 1:-1, 2:] - flux_x[:, 1:-1, :-2] + flux_y[:, 2:, 1:-1] - flux_y[:, :-2, 1:-1]
        height = height - 0.25 * div
        wide = pad_rim(height)
        grad_x = wide[:, 1:-1, 2:] - wide[:, 1:-1, :-2]
        grad_y = wide[:, 2:, 1:-1] - wide[:, :-2, 1:-1]
        east_new = east + 0.5 * (fcor * north - 0.5 * grad_x)
        north_new = north + 0.5 * (-fcor * east - 0.5 * grad_y)
        east, north = (east_new, north_new)
    lat_rows = jnp.arange(TLAT, dtype=jnp.int32)[:, None, None] * CLAT + obs_index // CLON
    lon_cols = jnp.arange(TLON, dtype=jnp.int32)[None, :, None] * CLON + obs_index % CLON
    hx = height[:, lat_rows, lon_cols].reshape(M, -1)
    valid = (jnp.arange(KOBS, dtype=jnp.int32)[None, None, :] < obs_count[:, :, None]).astype(jnp.float32).reshape(-1)
    sigma = obs_sd.reshape(-1) * (math.sqrt(NOBS) / 16.0)
    hmean = lax.optimization_barrier(jnp.mean(hx, axis=0))
    anomal = (hx - hmean) / (math.sqrt(M - 1) * sigma) * valid
    innov = (obs_value.reshape(-1) - hmean) / sigma * valid
    gram = jnp.dot(anomal, anomal.T, precision=lax.Precision.HIGHEST)
    proj = jnp.dot(anomal, innov, precision=lax.Precision.HIGHEST)
    eye = jnp.eye(M, dtype=jnp.float32)
    lower = jnp.linalg.cholesky(gram + eye)
    inv_lower = jax.scipy.linalg.solve_triangular(lower, eye, lower=True)
    weights = jax.scipy.linalg.cho_solve((lower, True), proj)
    transform = inv_lower.T + weights[:, None] / math.sqrt(M - 1)
    fields = jnp.stack([height, east, north])
    center = lax.optimization_barrier(jnp.mean(fields, axis=1, keepdims=True))
    mixed = jnp.einsum('nm,cnab->cmab', transform, fields - center, precision=lax.Precision.HIGHEST)
    return center + mixed
```

```python
import functools
import math

import jax
import jax.numpy as jnp
import numpy as np
from jax import lax
from jax.experimental import pallas as pl
from jax.experimental.pallas import tpu as pltpu
from jax.sharding import PartitionSpec as P

HI = lax.Precision.HIGHEST
CH = 8
PER = 8
ROWS = 8
COLS = 256
WIDE = 384
LANES = 128
EXT = 2 * COLS
BATH = EXT + 32
MSG = BATH + 8
VM = pltpu.VMEM


def roll(x, shift):
    return pltpu.roll(x, shift % x.shape[1], 1)


def ddx(x):
    return roll(x, -1) - roll(x, 1)


def lanes_of(shape):
    return lax.broadcasted_iota(jnp.int32, shape, 1)


def field_rows(lo, hi, c, q, i):
    rows = pl.ds(q * (CH * ROWS) + i, CH, stride=ROWS)
    return lo[c, rows, :], hi[c, rows, :]


def edges_kernel(lo, hi, bath, to_east, to_west, to_north, to_south):
    lane = lanes_of((CH, LANES))

    def chunk(q, carry):
        east = jnp.zeros((CH, LANES), jnp.float32)
        west = jnp.zeros((CH, LANES), jnp.float32)
        out = pl.ds(pl.multiple_of(q * CH, CH), CH)
        for c in range(4):
            for i in range(ROWS):
                if c < 3:
                    a, b = field_rows(lo, hi, c, q, i)
                else:
                    a = jnp.broadcast_to(bath[i : i + 1, :LANES], (CH, LANES))
                    b = jnp.broadcast_to(bath[i : i + 1, LANES:], (CH, LANES))
                spot = 4 * (c * ROWS + i)
                here = (lane >= spot) & (lane < spot + 4)
                west = jnp.where(here, roll(a, spot), west)
                east = jnp.where(here, roll(b, spot + 4), east)
        to_east[out, :] = east
        to_west[out, :] = west
        for i, ref in ((0, to_north), (ROWS - 1, to_south)):
            a, b = field_rows(lo, hi, 2, q, i)
            ref[out, :LANES] = a * bath[i : i + 1, :LANES]
            ref[out, LANES:] = b * bath[i : i + 1, LANES:]
        return carry

    lax.fori_loop(0, PER, chunk, 0)


def bath_rows(bath, from_east, from_west, wide_bath):
    lane = lanes_of((CH, LANES))
    e, w = from_east[0:CH, :], from_west[0:CH, :]
    for i in range(ROWS):
        spot = 4 * (3 * ROWS + i)
        tail = jnp.where(lane < 4, roll(e, -spot), roll(w, 124 - spot))
        wide_bath[i, :, :COLS] = jnp.broadcast_to(bath[i : i + 1, :], (CH, COLS))
        wide_bath[i, :, COLS:] = tail


def wide_rows(lo, hi, e, w, lane, q, c, i):
    a, b = field_rows(lo, hi, c, q, i)
    spot = 4 * (c * ROWS + i)
    tail = jnp.where(lane < 4, roll(e, -spot), roll(w, 124 - spot))
    return jnp.concatenate([a, b, tail], axis=1)


def border_kernel(nrows, lo, hi, bath, from_east, from_west, fcor, msg_n, msg_s, late_n, late_s, wide_bath):
    step = pl.program_id(0)
    base = lax.axis_index("lat") * nrows

    @pl.when(step == 0)
    def _():
        bath_rows(bath, from_east, from_west, wide_bath)
        for msg, r0, r1 in ((msg_n, 0, 1), (msg_s, ROWS - 1, ROWS - 2)):
            msg[EXT:MSG, :] = jnp.zeros((MSG - EXT, COLS), jnp.float32)
            msg[BATH : BATH + 1, :] = bath[r0 : r0 + 1, :]
            msg[BATH + 1 : BATH + 2, :] = bath[r1 : r1 + 1, :]
            msg[BATH + 2 : BATH + 3, :LANES] = wide_bath[r0, 0:1, COLS:]

    lane = lanes_of((CH, LANES))

    def chunk(q, carry):
        out = pl.ds(pl.multiple_of(q * CH, CH), CH)
        dst = pl.ds(pl.multiple_of(step * (CH * PER) + q * CH, CH), CH)
        dst_q = pl.ds(pl.multiple_of(COLS + step * (CH * PER) + q * CH, CH), CH)
        e, w = from_east[out, :], from_west[out, :]
        new = []
        for msg, late, first, sg, ext in (
            (msg_n, late_n, 0, 1, carry[0]),
            (msg_s, late_s, ROWS - 1, -1, carry[1]),
        ):
            rows = [first + sg * k for k in range(4)]
            H = [wide_bath[r] for r in rows]
            load = lambda c, k: wide_rows(lo, hi, e, w, lane, q, c, rows[k])
            h = [load(0, k) for k in range(3)]
            u = [load(1, k) for k in range(3)]
            v = [load(2, k) for k in range(4)]
            f0, f1 = fcor[base + rows[0]], fcor[base + rows[1]]
            fy = [H[k] * v[k] for k in range(4)]
            dfx = [ddx(H[k] * u[k]) for k in range(3)]
            h1a = h[1] - 0.25 * (dfx[1] + sg * (fy[2] - fy[0]))
            h1b = h[2] - 0.25 * (dfx[2] + sg * (fy[3] - fy[1]))
            part = h[0] - 0.25 * (dfx[0] + sg * fy[1])
            flux = H[0] * (v[0] - (0.5 * f0) * u[0] - (sg * 0.25) * h1a)
            uz = u[0] + (0.5 * f0) * v[0] - 0.25 * ddx(part)
            vz = v[1] - (0.5 * f1) * u[1] - (sg * 0.25) * (h1b - part)
            rest = part - 0.25 * (ddx(H[0] * uz) + sg * (H[1] * vz))
            msg[dst, :] = part[:, :COLS]
            msg[dst_q, :] = flux[:, :COLS]
            late[dst, :] = rest[:, :COLS]
            t = jnp.where(
                lane < 8,
                roll(fy[0][:, COLS:], 4),
                jnp.where(lane < 12, roll(part[:, COLS:], 10), roll(flux[:, COLS:], 14)),
            )
            t = pltpu.roll(t, q * 16, 1)
            new.append(jnp.where(lane // 16 == q, t, ext))
        return tuple(new)

    zero = jnp.zeros((CH, LANES), jnp.float32)
    exts = lax.fori_loop(0, PER, chunk, (zero, zero))
    for msg, ext in ((msg_n, exts[0]), (msg_s, exts[1])):
        msg[pl.ds(pl.multiple_of(EXT + step * CH, CH), CH), :LANES] = ext


def split(x, pieces):
    parts = []
    for k in range(pieces):
        p = x.astype(jnp.bfloat16)
        parts.append(p)
        if k + 1 < pieces:
            x = x - p.astype(jnp.float32)
    return parts


def dot(a, b, ca, cb):
    return lax.dot_general(
        a, b, (((ca,), (cb,)), ((), ())), precision=HI, preferred_element_type=jnp.float32
    )


def bdot(a, b):
    return jnp.dot(a, b, preferred_element_type=jnp.float32)


def forecast_kernel(
    nrows, ntiles, members, scale,
    lo, hi, bath, from_east, from_west, fcor, fy_n, fy_s, msg_n, msg_s, index, count, value, sd,
    out, sums, wide_bath, beyond, height,
):
    step = pl.program_id(0)
    tile = lax.axis_index("lat")
    base = tile * nrows
    has = (jnp.where(tile > 0, 1.0, 0.0), jnp.where(tile < ntiles - 1, 1.0, 0.0))

    @pl.when(step == 0)
    def _():
        bath_rows(bath, from_east, from_west, wide_bath)
        for k, msg in enumerate((msg_n, msg_s)):
            beyond[2 * k, :, :COLS] = jnp.broadcast_to(msg[BATH : BATH + 1, :], (CH, COLS))
            beyond[2 * k, :, COLS:] = jnp.broadcast_to(msg[BATH + 2 : BATH + 3, :LANES], (CH, LANES))
            beyond[2 * k + 1, :, :COLS] = jnp.broadcast_to(msg[BATH + 1 : BATH + 2, :], (CH, COLS))
            beyond[2 * k + 1, :, COLS:] = jnp.zeros((CH, LANES), jnp.float32)

    lane = lanes_of((CH, LANES))

    def chunk(q, carry):
        loc = pl.ds(pl.multiple_of(q * CH, CH), CH)
        dst = pl.ds(pl.multiple_of(step * (CH * PER) + q * CH, CH), CH)
        dst_q = pl.ds(pl.multiple_of(COLS + step * (CH * PER) + q * CH, CH), CH)
        e, w = from_east[loc, :], from_west[loc, :]
        load = lambda c, i: wide_rows(lo, hi, e, w, lane, q, c, i)
        H = [wide_bath[i] for i in range(ROWS)]
        f = [fcor[base + i] for i in range(ROWS)]
        h = [load(0, i) for i in range(ROWS)]
        u = [load(1, i) for i in range(ROWS)]
        v = [load(2, i) for i in range(ROWS)]
        ghost = []
        for msg, fy_msg in ((msg_n, fy_n), (msg_s, fy_s)):
            t = msg[pl.ds(pl.multiple_of(EXT + step * CH, CH), CH), :LANES]
            t = pltpu.roll(t, (LANES - q * 16) % LANES, 1)
            ghost.append((
                jnp.concatenate([fy_msg[loc, :], roll(t, -4)], axis=1),
                jnp.concatenate([msg[dst, :], roll(t, -10)], axis=1),
                jnp.concatenate([msg[dst_q, :], roll(t, -14)], axis=1),
            ))
        fy = [H[i] * v[i] for i in range(ROWS)]
        y = [ghost[0][0]] + fy + [ghost[1][0]]
        h1 = [h[i] - 0.25 * (ddx(H[i] * u[i]) + (y[i + 2] - y[i])) for i in range(ROWS)]
        eps = (-0.25 * fy[0], 0.25 * fy[-1])
        y = [has[0] * (ghost[0][1] + eps[0])] + h1 + [has[1] * (ghost[1][1] + eps[1])]
        u1 = [u[i] + (0.5 * f[i]) * v[i] - 0.25 * ddx(h1[i]) for i in range(ROWS)]
        v1 = [v[i] - (0.5 * f[i]) * u[i] - 0.25 * (y[i + 2] - y[i]) for i in range(ROWS)]
        fy = [H[i] * v1[i] for i in range(ROWS)]
        y = (
            [ghost[0][2] - 0.25 * (beyond[0] * h1[0])]
            + fy
            + [ghost[1][2] + 0.25 * (beyond[2] * h1[-1])]
        )
        h2 = [h1[i] - 0.25 * (ddx(H[i] * u1[i]) + (y[i + 2] - y[i])) for i in range(ROWS)]
        tail = []
        for k, sg, edge in ((0, -1, fy[0]), (1, 1, fy[-1])):
            bend = ddx(beyond[2 * k] * (-0.25 * ddx(eps[k])))
            tail.append(has[k] * (eps[k] - 0.25 * (bend - sg * edge + 0.25 * (beyond[2 * k + 1] * eps[k]))))
        y = [tail[0]] + h2 + [tail[1]]
        for i in range(ROWS):
            u2 = u1[i] + (0.5 * f[i]) * v1[i] - 0.25 * ddx(h2[i])
            v2 = v1[i] - (0.5 * f[i]) * u1[i] - 0.25 * (y[i + 2] - y[i])
            out[0, i, loc, :] = h2[i][:, :COLS]
            out[1, i, loc, :] = u2[:, :COLS]
            out[2, i, loc, :] = v2[:, :COLS]
            height[i, dst, :] = h2[i][:, :COLS]
        return carry

    lax.fori_loop(0, PER, chunk, 0)

    @pl.when(step == pl.num_programs(0) - 1)
    def _():
        slots = index.shape[1]
        sub = lax.broadcasted_iota(jnp.int32, (COLS, slots), 0)
        cell = jnp.broadcast_to(index[...], (COLS, slots))
        hx = jnp.zeros((members, slots), jnp.float32)
        for i in range(ROWS):
            pick = jnp.where(sub + i * COLS == cell, 1.0, 0.0).astype(jnp.bfloat16)
            for p in split(height[i], 3):
                hx = hx + bdot(p, pick)
        used = jnp.where(lanes_of((1, slots)) < count[0, 0], 1.0, 0.0)
        sigma = sd[...] * scale
        hmean = jnp.mean(hx, axis=0, keepdims=True)
        anom = (hx - hmean) * (used / (math.sqrt(members - 1) * sigma))
        innov = (value[...] - hmean) / sigma * used
        gram = dot(anom, anom, 1, 1)
        proj = dot(jnp.broadcast_to(innov, (8, slots)), anom, 1, 1)
        n = LANES
        ln, sb = lanes_of((n, n)), lax.broadcasted_iota(jnp.int32, (n, n), 0)
        last = gram[n:, n:]
        sums[0:n, :] = jnp.where(ln >= sb, gram[:n, :n], last)
        sums[n : 2 * n, :] = gram[:n, n:]
        sums[2 * n :, :] = jnp.zeros((16, n), jnp.float32)
        sums[2 * n : 2 * n + 1, :] = jnp.sum(jnp.where(ln == sb, last, 0.0), axis=0, keepdims=True)
        sums[2 * n + 1 : 2 * n + 2, :] = proj[0:1, :n]
        sums[2 * n + 2 : 2 * n + 3, :] = proj[0:1, n:]


def elim(a, dst, base):
    n = LANES
    groups = n // 8
    lane = lanes_of((8, n))
    sub = lax.broadcasted_iota(jnp.int32, (8, n), 0)
    A = [a[8 * g : 8 * g + 8, :] for g in range(groups)]
    X = [(lane == sub + 8 * g).astype(jnp.float32) for g in range(groups)]

    def body(it, carry):
        A, X = list(carry[:groups]), list(carry[groups:])
        for k in range(8):
            d = jnp.broadcast_to(A[0][k : k + 1, k : k + 1], (1, n))
            inv = 1.0 / d
            ra = A[0][k : k + 1, :] * inv
            rx = X[0][k : k + 1, :] * inv
            for g in range(groups):
                col = jnp.broadcast_to(A[g][:, k : k + 1], (8, n))
                if g == 0:
                    below = sub > k
                    scaled = jnp.where(sub == k, X[0] * lax.rsqrt(d), X[0])
                    A[0] = jnp.where(below, A[0] - col * ra, A[0])
                    X[0] = jnp.where(below, X[0] - col * rx, scaled)
                else:
                    A[g] = A[g] - col * ra
                    X[g] = X[g] - col * rx
        dst[pl.ds(pl.multiple_of(base + it * 8, 8), 8), :] = X[0]
        z = jnp.zeros((8, n), jnp.float32)
        A = [roll(A[g], -8) for g in range(1, groups)] + [z]
        return tuple(A) + tuple(X[1:]) + (z,)

    lax.fori_loop(0, groups, body, tuple(A) + tuple(X))


def factor_kernel(members, g_ref, mix, inverse):
    n = LANES
    lane, sub = lanes_of((n, n)), lax.broadcasted_iota(jnp.int32, (n, n), 0)
    both = g_ref[0:n, :]
    g12 = g_ref[n : 2 * n, :]
    tail = g_ref[2 * n : 2 * n + 8, :]
    eye = (lane == sub).astype(jnp.float32)
    up = jnp.where(lane >= sub, both, 0.0)
    low = jnp.where(lane < sub, both, 0.0)
    g11 = up + jnp.where(lane > sub, up, 0.0).T + eye
    g22 = low + low.T + jnp.where(lane == sub, jnp.broadcast_to(tail[0:1, :], (n, n)), 0.0) + eye
    elim(g11, inverse, 0)
    x11 = inverse[0:n, :]
    y12 = dot(x11, g12, 1, 0)
    elim(g22 - dot(y12, y12, 0, 0), inverse, n)
    x22 = inverse[n : 2 * n, :]
    x21 = -dot(x22, dot(y12, x11, 0, 0), 1, 0)
    p1 = jnp.broadcast_to(tail[1:2, :], (8, n))
    p2 = jnp.broadcast_to(tail[2:3, :], (8, n))
    q1 = dot(p1, x11, 1, 1)
    q2 = dot(p1, x21, 1, 1) + dot(p2, x22, 1, 1)
    c = 1.0 / math.sqrt(members - 1)
    w1 = (dot(q1, x11, 1, 0) + dot(q2, x21, 1, 0))[0:1, :] * c
    w2 = dot(q2, x22, 1, 0)[0:1, :] * c
    ws = jnp.sum(w1, axis=1, keepdims=True) + jnp.sum(w2, axis=1, keepdims=True)
    r = 1.0 / members
    s1 = (1.0 - ws - jnp.sum(x11, axis=1, keepdims=True)) * r
    s2 = (1.0 - ws - jnp.sum(x21, axis=1, keepdims=True) - jnp.sum(x22, axis=1, keepdims=True)) * r
    mix[0:n, 0:n] = x11 + (w1 + s1)
    mix[0:n, n:] = w2 + s1
    mix[n:, 0:n] = x21 + (w1 + s2)
    mix[n:, n:] = x22 + (w2 + s2)


def apply_kernel(mix, fields, late_n, late_s, out):
    high, low = split(mix[...], 2)
    wind = jnp.where(pl.program_id(0) == 2, 0.25, 0.0)
    for i in range(ROWS):
        x = fields[0, i]
        if i == 0:
            x = x + wind * late_n[...]
        if i == ROWS - 1:
            x = x - wind * late_s[...]
        a, b = split(x, 2)
        res = bdot(high, a) + (bdot(high, b) + bdot(low, a))
        out[0, pl.ds(i, x.shape[0], stride=ROWS), :] = res


def whole(shape):
    return pl.BlockSpec(shape, lambda *_: (0,) * len(shape))


def f32(*shape):
    return jax.ShapeDtypeStruct(shape, jnp.float32)


def flips(n, bit):
    return [(i, i ^ bit) for i in range(n)]


def bits(n):
    return [1 << k for k in range(n.bit_length() - 1)]


def total(x):
    nlon, nlat = lax.axis_size("lon"), lax.axis_size("lat")
    half = x.reshape(2, x.shape[0] // 2, x.shape[1])
    core = lax.axis_index("lon") % 2
    mine = lax.dynamic_index_in_dim(half, core, 0, keepdims=False)
    theirs = lax.dynamic_index_in_dim(half, 1 - core, 0, keepdims=False)
    y = mine + lax.ppermute(theirs, "lon", flips(nlon, 1))
    stages = []
    for axis, n, todo in (("lon", nlon, bits(nlon)[1:]), ("lat", nlat, bits(nlat)[1:] + bits(nlat)[:1])):
        for k in range(0, len(todo), 2):
            stages.append((axis, n, todo[k : k + 2]))
    for axis, n, todo in stages:
        hops = todo if len(todo) == 1 else [todo[0], todo[1], todo[0] | todo[1]]
        parts = [lax.ppermute(y, axis, flips(n, b)) for b in hops]
        for p in parts:
            y = y + p
    other = lax.ppermute(y, "lon", flips(nlon, 1))
    lo = jnp.where(core == 0, y, other)
    hi = jnp.where(core == 0, other, y)
    return jnp.concatenate([lo, hi], axis=0)


def shards(state, bathymetry, obs_index, obs_count, obs_value, obs_sd):
    members = state.shape[1]
    nlat, nlon = lax.axis_size("lat"), lax.axis_size("lon")
    slots = obs_index.shape[2]
    total_rows = ROWS * nlat
    fcor = np.sin(math.pi / 3.0 * ((np.arange(total_rows) + 0.5) / total_rows - 0.5)).astype(np.float32)
    flat = state.reshape(3, members * ROWS, COLS)
    blk = CH * PER
    grid = (members // blk,)
    state_specs = [
        pl.BlockSpec((3, blk * ROWS, LANES), lambda s: (0, s, 0)),
        pl.BlockSpec((3, blk * ROWS, LANES), lambda s: (0, s, 1)),
    ]
    thin = pl.BlockSpec((blk, LANES), lambda s: (s, 0))
    row = pl.BlockSpec((blk, COLS), lambda s: (s, 0))
    bath_spec = whole((ROWS, COLS))
    smem = pl.BlockSpec(memory_space=pltpu.SMEM)

    to_east, to_west, to_north, to_south = pl.pallas_call(
        edges_kernel,
        grid=grid,
        in_specs=state_specs + [bath_spec],
        out_specs=[thin, thin, row, row],
        out_shape=[f32(members, LANES)] * 2 + [f32(members, COLS)] * 2,
        name="edges",
    )(flat, flat, bathymetry)

    east = [(i, (i + 1) % nlon) for i in range(nlon)]
    west = [(j, i) for i, j in east]
    south = [(i, i + 1) for i in range(nlat - 1)]
    north = [(j, i) for i, j in south]
    from_west = lax.ppermute(to_east, "lon", east)
    from_east = lax.ppermute(to_west, "lon", west)
    fy_n = lax.ppermute(to_south, "lat", south)
    fy_s = lax.ppermute(to_north, "lat", north)

    msg_n, msg_s, late_n, late_s = pl.pallas_call(
        functools.partial(border_kernel, ROWS),
        grid=grid,
        in_specs=state_specs + [bath_spec, thin, thin, smem],
        out_specs=[whole((MSG, COLS))] * 2 + [whole((members, COLS))] * 2,
        out_shape=[f32(MSG, COLS)] * 2 + [f32(members, COLS)] * 2,
        scratch_shapes=[VM((ROWS, CH, WIDE), jnp.float32)],
        name="border",
    )(flat, flat, bathymetry, from_east, from_west, fcor)
    got_n = lax.ppermute(msg_s, "lat", south)
    got_s = lax.ppermute(msg_n, "lat", north)

    one = lambda x: x.reshape(1, slots)
    obs = whole((1, slots))
    fields, sums = pl.pallas_call(
        functools.partial(forecast_kernel, ROWS, nlat, members, math.sqrt(slots * nlat * nlon) / 16.0),
        grid=grid,
        in_specs=state_specs
        + [bath_spec, thin, thin, smem, row, row, whole((MSG, COLS)), whole((MSG, COLS))]
        + [obs, smem, obs, obs],
        out_specs=[pl.BlockSpec((3, ROWS, blk, COLS), lambda s: (0, 0, s, 0)), whole((272, LANES))],
        out_shape=[f32(3, ROWS, members, COLS), f32(272, LANES)],
        scratch_shapes=[
            VM((ROWS, CH, WIDE), jnp.float32),
            VM((4, CH, WIDE), jnp.float32),
            VM((ROWS, members, COLS), jnp.float32),
        ],
        name="forecast",
    )(
        flat, flat, bathymetry, from_east, from_west, fcor, fy_n, fy_s, got_n, got_s,
        one(obs_index), obs_count, one(obs_value), one(obs_sd),
    )

    sums, late_n, late_s = lax.optimization_barrier((sums, late_n, late_s))
    late_from_n = lax.ppermute(late_s, "lat", south)
    late_from_s = lax.ppermute(late_n, "lat", north)
    sums = total(sums)

    mix = pl.pallas_call(
        functools.partial(factor_kernel, members),
        out_shape=f32(members, members),
        in_specs=[pl.BlockSpec(memory_space=VM)],
        out_specs=pl.BlockSpec(memory_space=VM),
        scratch_shapes=[VM((members, LANES), jnp.float32)],
        name="factor",
    )(sums)

    half = pl.BlockSpec((members, LANES), lambda c, j: (0, j))
    analysis = pl.pallas_call(
        apply_kernel,
        grid=(3, COLS // LANES),
        in_specs=[
            whole((members, members)),
            pl.BlockSpec((1, ROWS, members, LANES), lambda c, j: (c, 0, 0, j)),
            half,
            half,
        ],
        out_specs=pl.BlockSpec((1, members * ROWS, LANES), lambda c, j: (c, 0, j)),
        out_shape=f32(3, members * ROWS, COLS),
        name="mix",
    )(mix, fields, late_from_n, late_from_s)
    return analysis.reshape(state.shape)


def solution(mesh):
    return jax.shard_map(
        shards,
        mesh=mesh,
        in_specs=(
            P(None, None, "lat", "lon"),
            P("lat", "lon"),
            P("lat", "lon", None),
            P("lat", "lon"),
            P("lat", "lon", None),
            P("lat", "lon", None),
        ),
        out_specs=P(None, None, "lat", "lon"),
        check_vma=False,
    )
```

```python
import functools
import math

import jax
import jax.numpy as jnp
import numpy as np
from jax import lax
from jax.experimental import pallas as pl
from jax.experimental.pallas import tpu as pltpu
from jax.sharding import PartitionSpec as P


HI = lax.Precision.HIGHEST
CH = 8
PER = 8
ROWS = 8
COLS = 256
WIDE = 384
LANES = 128
EXT = 2 * COLS
BATH = EXT + 32
MSG = BATH + 8
VM = pltpu.VMEM


def roll(x, shift):
    return pltpu.roll(x, shift % x.shape[1], 1)


def ddx(x):
    return roll(x, -1) - roll(x, 1)


def lanes_of(shape):
    return lax.broadcasted_iota(jnp.int32, shape, 1)


def field_rows(lo, hi, c, q, i):
    rows = pl.ds(q * (CH * ROWS) + i, CH, stride=ROWS)
    return lo[c, rows, :], hi[c, rows, :]


def edges_kernel(lo, hi, bath, to_east, to_west, to_north, to_south):
    lane = lanes_of((CH, LANES))

    def chunk(q, carry):
        east = jnp.zeros((CH, LANES), jnp.float32)
        west = jnp.zeros((CH, LANES), jnp.float32)
        out = pl.ds(pl.multiple_of(q * CH, CH), CH)
        for c in range(4):
            for i in range(ROWS):
                if c < 3:
                    a, b = field_rows(lo, hi, c, q, i)
                else:
                    a = jnp.broadcast_to(bath[i : i + 1, :LANES], (CH, LANES))
                    b = jnp.broadcast_to(bath[i : i + 1, LANES:], (CH, LANES))
                spot = 4 * (c * ROWS + i)
                here = (lane >= spot) & (lane < spot + 4)
                west = jnp.where(here, roll(a, spot), west)
                east = jnp.where(here, roll(b, spot + 4), east)
        to_east[out, :] = east
        to_west[out, :] = west
        for i, ref in ((0, to_north), (ROWS - 1, to_south)):
            a, b = field_rows(lo, hi, 2, q, i)
            ref[out, :LANES] = a * bath[i : i + 1, :LANES]
            ref[out, LANES:] = b * bath[i : i + 1, LANES:]
        return carry

    each(PER, chunk, 2)(0)


def bath_rows(bath, from_east, from_west, wide_bath):
    lane = lanes_of((CH, LANES))
    e, w = from_east[0:CH, :], from_west[0:CH, :]
    for i in range(ROWS):
        spot = 4 * (3 * ROWS + i)
        tail = jnp.where(lane < 4, roll(e, -spot), roll(w, 124 - spot))
        wide_bath[i, :, :COLS] = jnp.broadcast_to(bath[i : i + 1, :], (CH, COLS))
        wide_bath[i, :, COLS:] = tail


def wide_rows(lo, hi, e, w, lane, q, c, i):
    a, b = field_rows(lo, hi, c, q, i)
    spot = 4 * (c * ROWS + i)
    tail = jnp.where(lane < 4, roll(e, -spot), roll(w, 124 - spot))
    return jnp.concatenate([a, b, tail], axis=1)


def border_kernel(nrows, lo, hi, bath, from_east, from_west, fcor, msg_n, msg_s, late_n, late_s, wide_bath):
    step = pl.program_id(0)
    base = lax.axis_index("lat") * nrows

    @pl.when(step == 0)
    def _():
        bath_rows(bath, from_east, from_west, wide_bath)
        for msg, r0, r1 in ((msg_n, 0, 1), (msg_s, ROWS - 1, ROWS - 2)):
            msg[EXT:MSG, :] = jnp.zeros((MSG - EXT, COLS), jnp.float32)
            msg[BATH : BATH + 1, :] = bath[r0 : r0 + 1, :]
            msg[BATH + 1 : BATH + 2, :] = bath[r1 : r1 + 1, :]
            msg[BATH + 2 : BATH + 3, :LANES] = wide_bath[r0, 0:1, COLS:]

    lane = lanes_of((CH, LANES))

    def chunk(q, carry):
        out = pl.ds(pl.multiple_of(q * CH, CH), CH)
        dst = pl.ds(pl.multiple_of(step * (CH * PER) + q * CH, CH), CH)
        dst_q = pl.ds(pl.multiple_of(COLS + step * (CH * PER) + q * CH, CH), CH)
        e, w = from_east[out, :], from_west[out, :]
        new = []
        for msg, late, first, sg, ext in (
            (msg_n, late_n, 0, 1, carry[0]),
            (msg_s, late_s, ROWS - 1, -1, carry[1]),
        ):
            rows = [first + sg * k for k in range(4)]
            H = [wide_bath[r] for r in rows]
            load = lambda c, k: wide_rows(lo, hi, e, w, lane, q, c, rows[k])
            h = [load(0, k) for k in range(3)]
            u = [load(1, k) for k in range(3)]
            v = [load(2, k) for k in range(4)]
            f0, f1 = fcor[base + rows[0]], fcor[base + rows[1]]
            fy = [H[k] * v[k] for k in range(4)]
            dfx = [ddx(H[k] * u[k]) for k in range(3)]
            h1a = h[1] - 0.25 * (dfx[1] + sg * (fy[2] - fy[0]))
            h1b = h[2] - 0.25 * (dfx[2] + sg * (fy[3] - fy[1]))
            part = h[0] - 0.25 * (dfx[0] + sg * fy[1])
            flux = H[0] * (v[0] - (0.5 * f0) * u[0] - (sg * 0.25) * h1a)
            uz = u[0] + (0.5 * f0) * v[0] - 0.25 * ddx(part)
            vz = v[1] - (0.5 * f1) * u[1] - (sg * 0.25) * (h1b - part)
            rest = part - 0.25 * (ddx(H[0] * uz) + sg * (H[1] * vz))
            msg[dst, :] = part[:, :COLS]
            msg[dst_q, :] = flux[:, :COLS]
            late[dst, :] = rest[:, :COLS]
            t = jnp.where(
                lane < 8,
                roll(fy[0][:, COLS:], 4),
                jnp.where(lane < 12, roll(part[:, COLS:], 10), roll(flux[:, COLS:], 14)),
            )
            t = pltpu.roll(t, q * 16, 1)
            new.append(jnp.where(lane // 16 == q, t, ext))
        return tuple(new)

    zero = jnp.zeros((CH, LANES), jnp.float32)
    exts = each(PER, chunk, 4)((zero, zero))
    for msg, ext in ((msg_n, exts[0]), (msg_s, exts[1])):
        msg[pl.ds(pl.multiple_of(EXT + step * CH, CH), CH), :LANES] = ext


def split(x, pieces):
    parts = []
    for k in range(pieces):
        p = x.astype(jnp.bfloat16)
        parts.append(p)
        if k + 1 < pieces:
            x = x - p.astype(jnp.float32)
    return parts


def dot(a, b, ca, cb):
    return lax.dot_general(
        a, b, (((ca,), (cb,)), ((), ())), precision=HI, preferred_element_type=jnp.float32
    )


def bdot(a, b):
    return jnp.dot(a, b, preferred_element_type=jnp.float32)


def clip(limit):
    return pltpu.CompilerParams(vmem_limit_bytes=limit << 20)


def local_kernel(
    nrows, lo, hi, bath, from_east, from_west, fcor, index,
    out, flux_edge, height_edge, wind_edge, seen, wide_bath, height,
):
    step = pl.program_id(0)
    base = lax.axis_index("lat") * nrows

    @pl.when(step == 0)
    def _():
        bath_rows(bath, from_east, from_west, wide_bath)

    lane = lanes_of((CH, LANES))

    def across(y, i):
        if i == 0:
            return y[1]
        if i == ROWS - 1:
            return -y[i - 1]
        return y[i + 1] - y[i - 1]

    def chunk(q, carry):
        loc = pl.ds(pl.multiple_of(q * CH, CH), CH)
        dst = pl.ds(pl.multiple_of(step * (CH * PER) + q * CH, CH), CH)
        e, w = from_east[loc, :], from_west[loc, :]
        load = lambda c, i: wide_rows(lo, hi, e, w, lane, q, c, i)
        H = [wide_bath[i] for i in range(ROWS)]
        f = [fcor[base + i] for i in range(ROWS)]
        h = [load(0, i) for i in range(ROWS)]
        u = [load(1, i) for i in range(ROWS)]
        v = [load(2, i) for i in range(ROWS)]
        fy = [H[i] * v[i] for i in range(ROWS)]
        h1 = [h[i] - 0.25 * (ddx(H[i] * u[i]) + across(fy, i)) for i in range(ROWS)]
        u1 = [u[i] + (0.5 * f[i]) * v[i] - 0.25 * ddx(h1[i]) for i in range(ROWS)]
        v1 = [v[i] - (0.5 * f[i]) * u[i] - 0.25 * across(h1, i) for i in range(ROWS)]
        for k, i in ((0, 0), (1, ROWS - 1)):
            flux_edge[k, loc, :] = fy[i]
            height_edge[k, loc, :] = h1[i]
            wind_edge[k, loc, :] = v1[i][:, :COLS]
        fy = [H[i] * v1[i] for i in range(ROWS)]
        h2 = [h1[i] - 0.25 * (ddx(H[i] * u1[i]) + across(fy, i)) for i in range(ROWS)]
        for i in range(ROWS):
            u2 = u1[i] + (0.5 * f[i]) * v1[i] - 0.25 * ddx(h2[i])
            v2 = v1[i] - (0.5 * f[i]) * u1[i] - 0.25 * across(h2, i)
            out[0, i, loc, :] = h2[i][:, :COLS]
            out[1, i, loc, :] = u2[:, :COLS]
            out[2, i, loc, :] = v2[:, :COLS]
            height[i, dst, :] = h2[i][:, :COLS]
        return carry

    lax.fori_loop(0, PER, chunk, 0)

    @pl.when(step == pl.num_programs(0) - 1)
    def _():
        seen[...] = observe(index, [(i, height[i]) for i in range(ROWS)])


def observe(index, planes):
    slots = index.shape[1]
    sub = lax.broadcasted_iota(jnp.int32, (COLS, slots), 0)
    cell = jnp.broadcast_to(index[...], (COLS, slots))
    hx = jnp.zeros((planes[0][1].shape[0], slots), jnp.float32)
    for i, plane in planes:
        pick = jnp.where(sub + i * COLS == cell, 1.0, 0.0).astype(jnp.bfloat16)
        for p in split(plane, 3):
            hx = hx + bdot(p, pick)
    return hx


def beyond_rows(msgs, beyond):
    for k, msg in enumerate(msgs):
        beyond[2 * k, :, :COLS] = jnp.broadcast_to(msg[BATH : BATH + 1, :], (CH, COLS))
        beyond[2 * k, :, COLS:] = jnp.broadcast_to(msg[BATH + 2 : BATH + 3, :LANES], (CH, LANES))
        beyond[2 * k + 1, :, :COLS] = jnp.broadcast_to(msg[BATH + 1 : BATH + 2, :], (CH, COLS))
        beyond[2 * k + 1, :, COLS:] = jnp.zeros((CH, LANES), jnp.float32)


def edge_change(k, has, q, fy_msg, msg, flux_edge, height_edge, wide_bath, beyond):
    sg, e, n = ((-1, 0, 1), (1, ROWS - 1, ROWS - 2))[k]
    chunk = q % PER
    rows = pl.ds(pl.multiple_of(q * CH, CH), CH)
    rows_q = pl.ds(pl.multiple_of(COLS + q * CH, CH), CH)
    t = msg[pl.ds(pl.multiple_of(EXT + (q // PER) * CH, CH), CH), :LANES]
    t = pltpu.roll(t, (LANES - chunk * 16) % LANES, 1)
    g0 = jnp.concatenate([fy_msg[rows, :], roll(t, -4)], axis=1)
    part = jnp.concatenate([msg[rows, :], roll(t, -10)], axis=1)
    flux = jnp.concatenate([msg[rows_q, :], roll(t, -14)], axis=1)
    c = sg * 0.25
    eps = c * flux_edge[k, rows, :]
    dh1 = -c * g0
    du1 = -0.25 * ddx(dh1)
    dv_e = -c * (has * (part + eps))
    dv_n = -c * dh1
    h1 = height_edge[k, rows, :] + dh1
    g2 = flux + c * (beyond[2 * k] * h1)
    He, Hn = wide_bath[e], wide_bath[n]
    flow_n = Hn * dv_n
    a = dh1 - 0.25 * (ddx(He * du1) - sg * flow_n + sg * g2)
    b = -c * (He * dv_e)
    d = -c * flow_n
    return eps, du1, dv_e, dv_n, a, b, d


def sums_kernel(
    ntiles, members, scale,
    bath, from_east, from_west, fy_n, fy_s, msg_n, msg_s, flux_edge, height_edge, seen, index, count, value, sd,
    sums, wide_bath, beyond, change,
):
    tile = lax.axis_index("lat")
    has = (jnp.where(tile > 0, 1.0, 0.0), jnp.where(tile < ntiles - 1, 1.0, 0.0))
    bath_rows(bath, from_east, from_west, wide_bath)
    beyond_rows((msg_n, msg_s), beyond)
    slots = index.shape[1]

    def chunk(q, carry):
        dst = pl.ds(pl.multiple_of(q * CH, CH), CH)
        for k, fy, msg in ((0, fy_n, msg_n), (1, fy_s, msg_s)):
            new = edge_change(k, has[k], q, fy, msg, flux_edge, height_edge, wide_bath, beyond)
            for j in range(3):
                change[3 * k + j, dst, :] = new[4 + j][:, :COLS]
        return carry

    each(members // CH, chunk, 4)(0)
    rows = (0, 1, 2, ROWS - 1, ROWS - 2, ROWS - 3)
    hx = seen[...] + observe(index, [(r, change[j]) for j, r in enumerate(rows)])
    used = jnp.where(lanes_of((1, slots)) < count[0, 0], 1.0, 0.0)
    sigma = sd[...] * scale
    hmean = jnp.mean(hx, axis=0, keepdims=True)
    anom = (hx - hmean) * (used / (math.sqrt(members - 1) * sigma))
    innov = (value[...] - hmean) / sigma * used
    gram = dot(anom, anom, 1, 1)
    proj = dot(jnp.broadcast_to(innov, (8, slots)), anom, 1, 1)
    n = LANES
    ln, sb = lanes_of((n, n)), lax.broadcasted_iota(jnp.int32, (n, n), 0)
    last = gram[n:, n:]
    sums[0:n, :] = jnp.where(ln >= sb, gram[:n, :n], last)
    sums[n : 2 * n, :] = gram[:n, n:]
    sums[2 * n :, :] = jnp.zeros((16, n), jnp.float32)
    sums[2 * n : 2 * n + 1, :] = jnp.sum(jnp.where(ln == sb, last, 0.0), axis=0, keepdims=True)
    sums[2 * n + 1 : 2 * n + 2, :] = proj[0:1, :n]
    sums[2 * n + 2 : 2 * n + 3, :] = proj[0:1, n:]


def complete_kernel(
    nrows, ntiles, block,
    bath, from_east, from_west, fcor, fy_n, fy_s, msg_n, msg_s, flux_edge, height_edge, wind_edge, fields,
    out, wide_bath, beyond,
):
    tile = lax.axis_index("lat")
    base = tile * nrows
    has = (jnp.where(tile > 0, 1.0, 0.0), jnp.where(tile < ntiles - 1, 1.0, 0.0))
    bath_rows(bath, from_east, from_west, wide_bath)
    beyond_rows((msg_n, msg_s), beyond)

    def chunk(q, carry):
        loc = pl.ds(pl.multiple_of(q * CH, CH), CH)
        full = block * PER + q
        rows = pl.ds(pl.multiple_of(full * CH, CH), CH)
        for k, sg, e, fy, msg in ((0, -1, 0, fy_n, msg_n), (1, 1, ROWS - 1, fy_s, msg_s)):
            eps, du1, dv_e, dv_n, a, b, d = edge_change(
                k, has[k], full, fy, msg, flux_edge, height_edge, wide_bath, beyond
            )
            c = sg * 0.25
            flow = wide_bath[e] * dv_e
            flow = flow[:, :COLS] + wide_bath[e][:, :COLS] * wind_edge[k, rows, :]
            bend = ddx(beyond[2 * k] * (-0.25 * ddx(eps))) + 0.25 * (beyond[2 * k + 1] * eps)
            g3 = has[k] * (eps[:, :COLS] - 0.25 * (bend[:, :COLS] - sg * flow))
            cut = lambda x: x[:, :COLS]
            f0, f1 = 0.5 * fcor[base + e], 0.5 * fcor[base + e - sg]
            r = [e - sg * j for j in range(4)]
            upd = (
                (0, r[0], cut(a)),
                (0, r[1], cut(b)),
                (0, r[2], cut(d)),
                (1, r[0], cut(du1 + f0 * dv_e - 0.25 * ddx(a))),
                (1, r[1], cut(f1 * dv_n - 0.25 * ddx(b))),
                (1, r[2], cut(-0.25 * ddx(d))),
                (2, r[0], cut(dv_e - f0 * du1) - c * (g3 - cut(b))),
                (2, r[1], cut(dv_n - c * (a - d))),
                (2, r[2], cut(-c * b)),
                (2, r[3], cut(-c * d)),
            )
            for i, j, x in upd:
                out[i, j, loc, :] = fields[i, j, loc, :] + x
        return carry

    for i in range(2):
        for j in (3, 4):
            out[i, j] = fields[i, j]
    each(PER, chunk, 4)(0)


def elim(a, dst, base):
    n = LANES
    groups = n // 8
    lane = lanes_of((8, n))
    sub = lax.broadcasted_iota(jnp.int32, (8, n), 0)
    A = [a[8 * g : 8 * g + 8, :] for g in range(groups)]
    X = [(lane == sub + 8 * g).astype(jnp.float32) for g in range(groups)]

    def body(live, it, carry):
        A, X = list(carry[:live]), list(carry[live:])
        cols = [[jnp.broadcast_to(A[g][:, k : k + 1], (8, n)) for k in range(8)] for g in range(live)]
        C, P, Z = cols[0], A[0], X[0]
        rows = Z
        for k in range(8):
            pick = lambda x: jnp.broadcast_to(x[k : k + 1, :], (8, n))
            here = sub == k
            d = pick(C[k])
            inv = 1.0 / d
            rows = jnp.where(here, Z * lax.rsqrt(d), rows)
            ra, rx = pick(P) * inv, pick(Z) * inv
            for j in range(k + 1, 8):
                rc = pick(C[j]) * inv
                C[j] = jnp.where(here, rc, C[j] - C[k] * rc)
            P = jnp.where(here, ra, P - C[k] * ra)
            Z = jnp.where(here, rx, Z - C[k] * rx)
        dst[pl.ds(pl.multiple_of(base + it * 8, 8), 8), :] = rows
        for k in range(8):
            rp, rz = (jnp.broadcast_to(x[k : k + 1, :], (8, n)) for x in (P, Z))
            for g in range(1, live):
                A[g] = A[g] - cols[g][k] * rp
                X[g] = X[g] - cols[g][k] * rz
        z = jnp.zeros((8, n), jnp.float32)
        A = [roll(A[g], -8) for g in range(1, live)] + [z]
        return tuple(A) + tuple(X[1:]) + (z,)

    seg = 4
    for first in range(0, groups, seg):
        live = groups - first
        out = lax.fori_loop(first, first + seg, functools.partial(body, live), tuple(A) + tuple(X))
        A, X = list(out[: live - seg]), list(out[live : 2 * live - seg])


def factor_kernel(members, g_ref, mix, inverse):
    n = LANES
    lane, sub = lanes_of((n, n)), lax.broadcasted_iota(jnp.int32, (n, n), 0)
    both = g_ref[0:n, :]
    g12 = g_ref[n : 2 * n, :]
    tail = g_ref[2 * n : 2 * n + 8, :]
    eye = (lane == sub).astype(jnp.float32)
    up = jnp.where(lane >= sub, both, 0.0)
    low = jnp.where(lane < sub, both, 0.0)
    g11 = up + jnp.where(lane > sub, up, 0.0).T + eye
    g22 = low + low.T + jnp.where(lane == sub, jnp.broadcast_to(tail[0:1, :], (n, n)), 0.0) + eye
    elim(g11, inverse, 0)
    x11 = inverse[0:n, :]
    y12 = dot(x11, g12, 1, 0)
    elim(g22 - dot(y12, y12, 0, 0), inverse, n)
    x22 = inverse[n : 2 * n, :]
    x21 = -dot(x22, dot(y12, x11, 0, 0), 1, 0)
    p1 = jnp.broadcast_to(tail[1:2, :], (8, n))
    p2 = jnp.broadcast_to(tail[2:3, :], (8, n))
    q1 = dot(p1, x11, 1, 1)
    q2 = dot(p1, x21, 1, 1) + dot(p2, x22, 1, 1)
    c = 1.0 / math.sqrt(members - 1)
    w1 = (dot(q1, x11, 1, 0) + dot(q2, x21, 1, 0))[0:1, :] * c
    w2 = dot(q2, x22, 1, 0)[0:1, :] * c
    ws = jnp.sum(w1, axis=1, keepdims=True) + jnp.sum(w2, axis=1, keepdims=True)
    r = 1.0 / members
    s1 = (1.0 - ws - jnp.sum(x11, axis=1, keepdims=True)) * r
    s2 = (1.0 - ws - jnp.sum(x21, axis=1, keepdims=True) - jnp.sum(x22, axis=1, keepdims=True)) * r
    mix[0:n, 0:n] = x11 + (w1 + s1)
    mix[0:n, n:] = w2 + s1
    mix[n:, 0:n] = x21 + (w1 + s2)
    mix[n:, n:] = x22 + (w2 + s2)


def apply_kernel(mix, fields, late_n, late_s, out):
    high, low = split(mix[...], 2)
    wind = jnp.where(pl.program_id(0) == 2, 0.25, 0.0)
    for i in range(ROWS):
        x = fields[0, i]
        if i == 0:
            x = x + wind * late_n[...]
        if i == ROWS - 1:
            x = x - wind * late_s[...]
        a, b = split(x, 2)
        res = bdot(high, a) + (bdot(high, b) + bdot(low, a))
        out[0, pl.ds(i, x.shape[0], stride=ROWS), :] = res


def each(trips, fn, together):
    def turn(t, carry):
        for j in range(together):
            carry = fn(t * together + j, carry)
        return carry

    return lambda init: lax.fori_loop(0, trips // together, turn, init)


def whole(shape):
    return pl.BlockSpec(shape, lambda *_: (0,) * len(shape))


def f32(*shape):
    return jax.ShapeDtypeStruct(shape, jnp.float32)


def flips(n, bit):
    return [(i, i ^ bit) for i in range(n)]


def bits(n):
    return [1 << k for k in range(n.bit_length() - 1)]


def total(x):
    nlon, nlat = lax.axis_size("lon"), lax.axis_size("lat")
    half = x.reshape(2, x.shape[0] // 2, x.shape[1])
    core = lax.axis_index("lon") % 2
    mine = lax.dynamic_index_in_dim(half, core, 0, keepdims=False)
    theirs = lax.dynamic_index_in_dim(half, 1 - core, 0, keepdims=False)
    y = mine + lax.ppermute(theirs, "lon", flips(nlon, 1))
    stages = []
    for axis, n, todo in (("lon", nlon, bits(nlon)[1:]), ("lat", nlat, bits(nlat)[1:] + bits(nlat)[:1])):
        for k in range(0, len(todo), 2):
            stages.append((axis, n, todo[k : k + 2]))
    for axis, n, todo in stages:
        hops = todo if len(todo) == 1 else [todo[0], todo[1], todo[0] | todo[1]]
        parts = [lax.ppermute(y, axis, flips(n, b)) for b in hops]
        for p in parts:
            y = y + p
    other = lax.ppermute(y, "lon", flips(nlon, 1))
    lo = jnp.where(core == 0, y, other)
    hi = jnp.where(core == 0, other, y)
    return jnp.concatenate([lo, hi], axis=0)


def body(state, bathymetry, obs_index, obs_count, obs_value, obs_sd):
    members = state.shape[1]
    nlat, nlon = lax.axis_size("lat"), lax.axis_size("lon")
    slots = obs_index.shape[2]
    total_rows = ROWS * nlat
    fcor = np.sin(math.pi / 3.0 * ((np.arange(total_rows) + 0.5) / total_rows - 0.5)).astype(np.float32)
    flat = pltpu.with_memory_space_constraint(state.reshape(3, members * ROWS, COLS), pltpu.HBM)
    blk = CH * PER
    grid = (members // blk,)
    state_specs = [
        pl.BlockSpec((3, blk * ROWS, LANES), lambda s: (0, s, 0)),
        pl.BlockSpec((3, blk * ROWS, LANES), lambda s: (0, s, 1)),
    ]
    thin = pl.BlockSpec((blk, LANES), lambda s: (s, 0))
    row = pl.BlockSpec((blk, COLS), lambda s: (s, 0))
    bath_spec = whole((ROWS, COLS))
    smem = pl.BlockSpec(memory_space=pltpu.SMEM)

    to_east, to_west, to_north, to_south = pl.pallas_call(
        edges_kernel,
        grid=grid,
        in_specs=state_specs + [bath_spec],
        out_specs=[thin, thin, row, row],
        out_shape=[f32(members, LANES)] * 2 + [f32(members, COLS)] * 2,
        compiler_params=clip(24),
        name="edges",
    )(flat, flat, bathymetry)

    east = [(i, (i + 1) % nlon) for i in range(nlon)]
    west = [(j, i) for i, j in east]
    south = [(i, i + 1) for i in range(nlat - 1)]
    north = [(j, i) for i, j in south]
    from_west = lax.ppermute(to_east, "lon", east)
    from_east = lax.ppermute(to_west, "lon", west)
    fy_n = lax.ppermute(to_south, "lat", south)
    fy_s = lax.ppermute(to_north, "lat", north)

    msg_n, msg_s, late_n, late_s = pl.pallas_call(
        functools.partial(border_kernel, ROWS),
        grid=grid,
        in_specs=state_specs + [bath_spec, thin, thin, smem],
        out_specs=[whole((MSG, COLS))] * 2 + [whole((members, COLS))] * 2,
        out_shape=[f32(MSG, COLS)] * 2 + [f32(members, COLS)] * 2,
        scratch_shapes=[VM((ROWS, CH, WIDE), jnp.float32)],
        compiler_params=clip(24),
        name="border",
    )(flat, flat, bathymetry, from_east, from_west, fcor)
    got_n = lax.ppermute(msg_s, "lat", south)
    got_s = lax.ppermute(msg_n, "lat", north)

    one = lambda x: x.reshape(1, slots)
    obs = whole((1, slots))
    edge = whole((2, members, WIDE))
    blocks = members // blk
    wide_scratch = VM((ROWS, CH, WIDE), jnp.float32)
    beyond_scratch = VM((4, CH, WIDE), jnp.float32)
    fields, flux_edge, height_edge, wind_edge, seen = pl.pallas_call(
        functools.partial(local_kernel, ROWS),
        grid=grid,
        in_specs=state_specs + [bath_spec, thin, thin, smem, obs],
        out_specs=[
            pl.BlockSpec((3, ROWS, blk, COLS), lambda s: (0, 0, s, 0)),
            pl.BlockSpec((2, blk, WIDE), lambda s: (0, s, 0)),
            pl.BlockSpec((2, blk, WIDE), lambda s: (0, s, 0)),
            pl.BlockSpec((2, blk, COLS), lambda s: (0, s, 0)),
            whole((members, slots)),
        ],
        out_shape=[
            pltpu.HBM((3, ROWS, members, COLS), jnp.float32), f32(2, members, WIDE), f32(2, members, WIDE),
            f32(2, members, COLS), f32(members, slots),
        ],
        scratch_shapes=[wide_scratch, VM((ROWS, members, COLS), jnp.float32)],
        compiler_params=clip(24),
        name="local",
    )(flat, flat, bathymetry, from_east, from_west, fcor, one(obs_index))

    head = whole((CH, LANES))
    got = (fy_n, fy_s, got_n, got_s, flux_edge, height_edge)
    got_specs = [whole((members, COLS))] * 2 + [whole((MSG, COLS))] * 2 + [edge, edge]
    sums = pl.pallas_call(
        functools.partial(sums_kernel, nlat, members, math.sqrt(slots * nlat * nlon) / 16.0),
        grid=(1,),
        in_specs=[bath_spec, head, head] + got_specs + [whole((members, slots)), obs, smem, obs, obs],
        out_specs=whole((272, LANES)),
        out_shape=f32(272, LANES),
        scratch_shapes=[wide_scratch, beyond_scratch, VM((6, members, COLS), jnp.float32)],
        compiler_params=clip(24),
        name="sums",
    )(
        bathymetry, from_east, from_west, *got, seen,
        one(obs_index), obs_count, one(obs_value), one(obs_sd),
    )

    for k in range(blocks):
        part = pl.BlockSpec((3, ROWS, blk, COLS), lambda s, k=k: (0, 0, k, 0))
        fields = pl.pallas_call(
            functools.partial(complete_kernel, ROWS, nlat, k),
            grid=(1,),
            in_specs=[bath_spec, head, head, smem] + got_specs + [whole((2, members, COLS)), part],
            out_specs=part,
            out_shape=pltpu.HBM((3, ROWS, members, COLS), jnp.float32),
            scratch_shapes=[wide_scratch, beyond_scratch],
            input_output_aliases={11: 0},
            compiler_params=clip(24),
            name="complete",
        )(bathymetry, from_east, from_west, fcor, *got, wind_edge, fields)

    sums, late_n, late_s = lax.optimization_barrier((total(sums), late_n, late_s))
    late_from_n = lax.ppermute(late_s, "lat", south)
    late_from_s = lax.ppermute(late_n, "lat", north)

    mix = pl.pallas_call(
        functools.partial(factor_kernel, members),
        out_shape=f32(members, members),
        in_specs=[pl.BlockSpec(memory_space=VM)],
        out_specs=pl.BlockSpec(memory_space=VM),
        scratch_shapes=[VM((members, LANES), jnp.float32)],
        compiler_params=clip(8),
        name="factor",
    )(sums)

    half = pl.BlockSpec((members, LANES), lambda c, j: (0, j))
    analysis = pl.pallas_call(
        apply_kernel,
        grid=(3, COLS // LANES),
        in_specs=[
            whole((members, members)),
            pl.BlockSpec((1, ROWS, members, LANES), lambda c, j: (c, 0, 0, j)),
            half,
            half,
        ],
        out_specs=pl.BlockSpec((1, members * ROWS, LANES), lambda c, j: (c, 0, j)),
        out_shape=f32(3, members * ROWS, COLS),
        compiler_params=clip(24),
        name="mix",
    )(mix, fields, late_from_n, late_from_s)
    return analysis.reshape(state.shape)


def solution(mesh):
    return jax.shard_map(
        body,
        mesh=mesh,
        in_specs=(
            P(None, None, "lat", "lon"),
            P("lat", "lon"),
            P("lat", "lon", None),
            P("lat", "lon"),
            P("lat", "lon", None),
            P("lat", "lon", None),
        ),
        out_specs=P(None, None, "lat", "lon"),
        check_vma=False,
    )
```

```python
import functools
import math

import jax
import jax.numpy as jnp
import numpy as np
from jax import lax
from jax.experimental import pallas as pl
from jax.experimental.pallas import tpu as pltpu
from jax.sharding import PartitionSpec as P


HI = lax.Precision.HIGHEST
CH = 8
PER = 8
ROWS = 8
COLS = 256
WIDE = 384
LANES = 128
EXT = 2 * COLS
BATH = EXT + 32
MSG = BATH + 8
VM = pltpu.VMEM


def each(trips, fn, together):
    def turn(t, carry):
        for j in range(together):
            carry = fn(t * together + j, carry)
        return carry

    return lambda init: lax.fori_loop(0, trips // together, turn, init)


def roll(x, shift):
    return pltpu.roll(x, shift % x.shape[1], 1)


def ddx(x):
    return roll(x, -1) - roll(x, 1)


def lanes_of(shape):
    return lax.broadcasted_iota(jnp.int32, shape, 1)


def field_rows(lo, hi, c, q, i):
    rows = pl.ds(q * (CH * ROWS) + i, CH, stride=ROWS)
    return lo[c, rows, :], hi[c, rows, :]


def flux_kernel(lo, hi, bath, to_north, to_south):
    def chunk(q, carry):
        out = pl.ds(pl.multiple_of(q * CH, CH), CH)
        for i, ref in ((0, to_north), (ROWS - 1, to_south)):
            a, b = field_rows(lo, hi, 0, q, i)
            ref[out, :LANES] = a * bath[i : i + 1, :LANES]
            ref[out, LANES:] = b * bath[i : i + 1, LANES:]
        return carry

    each(PER, chunk, 4)(0)


def edges_kernel(lo, hi, bath, to_east, to_west):
    lane = lanes_of((CH, LANES))
    first = jnp.zeros((CH, LANES), jnp.float32)
    last = jnp.zeros((CH, LANES), jnp.float32)
    place = lambda spot: (lane >= spot) & (lane < spot + 4)
    for i in range(ROWS):
        spot = 4 * (3 * ROWS + i)
        a = jnp.broadcast_to(bath[i : i + 1, :LANES], (CH, LANES))
        b = jnp.broadcast_to(bath[i : i + 1, LANES:], (CH, LANES))
        first = jnp.where(place(spot), roll(a, spot), first)
        last = jnp.where(place(spot), roll(b, spot + 4), last)

    def chunk(q, carry):
        west, east = first, last
        out = pl.ds(pl.multiple_of(q * CH, CH), CH)
        for c in range(3):
            for i in range(ROWS):
                a, b = field_rows(lo, hi, c, q, i)
                spot = 4 * (c * ROWS + i)
                west = jnp.where(place(spot), roll(a, spot), west)
                east = jnp.where(place(spot), roll(b, spot + 4), east)
        to_east[out, :] = east
        to_west[out, :] = west
        return carry

    each(PER, chunk, 2)(0)


def bath_rows(bath, from_east, from_west, wide_bath):
    lane = lanes_of((CH, LANES))
    e, w = from_east[0:CH, :], from_west[0:CH, :]
    for i in range(ROWS):
        spot = 4 * (3 * ROWS + i)
        tail = jnp.where(lane < 4, roll(e, -spot), roll(w, 124 - spot))
        wide_bath[i, :, :COLS] = jnp.broadcast_to(bath[i : i + 1, :], (CH, COLS))
        wide_bath[i, :, COLS:] = tail


def wide_rows(lo, hi, e, w, lane, q, c, i):
    a, b = field_rows(lo, hi, c, q, i)
    spot = 4 * (c * ROWS + i)
    tail = jnp.where(lane < 4, roll(e, -spot), roll(w, 124 - spot))
    return jnp.concatenate([a, b, tail], axis=1)


def border_kernel(nrows, lo, hi, bath, from_east, from_west, fcor, msg_n, msg_s, wide_bath):
    step = pl.program_id(0)
    base = lax.axis_index("lat") * nrows

    @pl.when(step == 0)
    def _():
        bath_rows(bath, from_east, from_west, wide_bath)
        for msg, r0, r1 in ((msg_n, 0, 1), (msg_s, ROWS - 1, ROWS - 2)):
            msg[EXT:MSG, :] = jnp.zeros((MSG - EXT, COLS), jnp.float32)
            msg[BATH : BATH + 1, :] = bath[r0 : r0 + 1, :]
            msg[BATH + 1 : BATH + 2, :] = bath[r1 : r1 + 1, :]
            msg[BATH + 2 : BATH + 3, :LANES] = wide_bath[r0, 0:1, COLS:]

    lane = lanes_of((CH, LANES))

    def chunk(q, carry):
        out = pl.ds(pl.multiple_of(q * CH, CH), CH)
        dst = pl.ds(pl.multiple_of(step * (CH * PER) + q * CH, CH), CH)
        dst_q = pl.ds(pl.multiple_of(COLS + step * (CH * PER) + q * CH, CH), CH)
        e, w = from_east[out, :], from_west[out, :]
        new = []
        for msg, first, sg, ext in ((msg_n, 0, 1, carry[0]), (msg_s, ROWS - 1, -1, carry[1])):
            rows = [first + sg * k for k in range(3)]
            H = [wide_bath[r] for r in rows]
            load = lambda c, k: wide_rows(lo, hi, e, w, lane, q, c, rows[k])
            h = [load(0, k) for k in range(2)]
            u = [load(1, k) for k in range(2)]
            v = [load(2, k) for k in range(3)]
            f0 = fcor[base + rows[0]]
            fy = [H[k] * v[k] for k in range(3)]
            dfx = [ddx(H[k] * u[k]) for k in range(2)]
            h1a = h[1] - 0.25 * (dfx[1] + sg * (fy[2] - fy[0]))
            part = h[0] - 0.25 * (dfx[0] + sg * fy[1])
            flux = H[0] * (v[0] - (0.5 * f0) * u[0] - (sg * 0.25) * h1a)
            msg[dst, :] = part[:, :COLS]
            msg[dst_q, :] = flux[:, :COLS]
            t = jnp.where(
                lane < 8,
                roll(fy[0][:, COLS:], 4),
                jnp.where(lane < 12, roll(part[:, COLS:], 10), roll(flux[:, COLS:], 14)),
            )
            t = pltpu.roll(t, q * 16, 1)
            new.append(jnp.where(lane // 16 == q, t, ext))
        return tuple(new)

    zero = jnp.zeros((CH, LANES), jnp.float32)
    exts = each(PER, chunk, 4)((zero, zero))
    for msg, ext in ((msg_n, exts[0]), (msg_s, exts[1])):
        msg[pl.ds(pl.multiple_of(EXT + step * CH, CH), CH), :LANES] = ext


def split(x, pieces):
    parts = []
    for k in range(pieces):
        p = x.astype(jnp.bfloat16)
        parts.append(p)
        if k + 1 < pieces:
            x = x - p.astype(jnp.float32)
    return parts


def dot(a, b, ca, cb):
    return lax.dot_general(
        a, b, (((ca,), (cb,)), ((), ())), precision=HI, preferred_element_type=jnp.float32
    )


def bdot(a, b):
    return jnp.dot(a, b, preferred_element_type=jnp.float32)


def clip(limit):
    return pltpu.CompilerParams(vmem_limit_bytes=limit << 20)


def local_kernel(
    nrows, lo, hi, wide_bath, from_east, from_west, fcor, index,
    out, flux_edge, height_edge, wind_edge, seen, late_n, late_s, height,
):
    step = pl.program_id(0)
    base = lax.axis_index("lat") * nrows
    lane = lanes_of((CH, LANES))

    def across(y, i):
        if i == 0:
            return y[1]
        if i == ROWS - 1:
            return -y[i - 1]
        return y[i + 1] - y[i - 1]

    def chunk(q, carry):
        loc = pl.ds(pl.multiple_of(q * CH, CH), CH)
        dst = pl.ds(pl.multiple_of(step * (CH * PER) + q * CH, CH), CH)
        e, w = from_east[loc, :], from_west[loc, :]
        load = lambda c, i: wide_rows(lo, hi, e, w, lane, q, c, i)
        H = [wide_bath[i] for i in range(ROWS)]
        f = [fcor[base + i] for i in range(ROWS)]
        h = [load(0, i) for i in range(ROWS)]
        u = [load(1, i) for i in range(ROWS)]
        v = [load(2, i) for i in range(ROWS)]
        fy = [H[i] * v[i] for i in range(ROWS)]
        h1 = [h[i] - 0.25 * (ddx(H[i] * u[i]) + across(fy, i)) for i in range(ROWS)]
        u1 = [u[i] + (0.5 * f[i]) * v[i] - 0.25 * ddx(h1[i]) for i in range(ROWS)]
        v1 = [v[i] - (0.5 * f[i]) * u[i] - 0.25 * across(h1, i) for i in range(ROWS)]
        for k, i in ((0, 0), (1, ROWS - 1)):
            flux_edge[k, loc, :] = fy[i]
            height_edge[k, loc, :] = h1[i]
            wind_edge[k, loc, :] = v1[i][:, :COLS]
        fy = [H[i] * v1[i] for i in range(ROWS)]
        h2 = [h1[i] - 0.25 * (ddx(H[i] * u1[i]) + across(fy, i)) for i in range(ROWS)]
        for i in range(ROWS):
            u2 = u1[i] + (0.5 * f[i]) * v1[i] - 0.25 * ddx(h2[i])
            v2 = v1[i] - (0.5 * f[i]) * u1[i] - 0.25 * across(h2, i)
            out[0, i, loc, :] = h2[i][:, :COLS]
            out[1, i, loc, :] = u2[:, :COLS]
            out[2, i, loc, :] = v2[:, :COLS]
            height[i, dst, :] = h2[i][:, :COLS]
        late_n[loc, :] = h2[0][:, :COLS]
        late_s[loc, :] = h2[-1][:, :COLS]
        return carry

    lax.fori_loop(0, PER, chunk, 0)

    @pl.when(step == pl.num_programs(0) - 1)
    def _():
        seen[...] = observe(index, [(i, height[i]) for i in range(ROWS)])


def observe(index, planes):
    slots = index.shape[1]
    sub = lax.broadcasted_iota(jnp.int32, (COLS, slots), 0)
    cell = jnp.broadcast_to(index[...], (COLS, slots))
    hx = jnp.zeros((planes[0][1].shape[0], slots), jnp.float32)
    for i, plane in planes:
        pick = jnp.where(sub + i * COLS == cell, 1.0, 0.0).astype(jnp.bfloat16)
        for p in split(plane, 3):
            hx = hx + bdot(p, pick)
    return hx


def beyond_rows(msgs, beyond):
    for k, msg in enumerate(msgs):
        beyond[2 * k, :, :COLS] = jnp.broadcast_to(msg[BATH : BATH + 1, :], (CH, COLS))
        beyond[2 * k, :, COLS:] = jnp.broadcast_to(msg[BATH + 2 : BATH + 3, :LANES], (CH, LANES))
        beyond[2 * k + 1, :, :COLS] = jnp.broadcast_to(msg[BATH + 1 : BATH + 2, :], (CH, COLS))
        beyond[2 * k + 1, :, COLS:] = jnp.zeros((CH, LANES), jnp.float32)


def edge_change(k, has, q, chunk, fy_row, part_row, flux_row, ext, flux_edge, height_edge, wide_bath, beyond):
    sg, e, n = ((-1, 0, 1), (1, ROWS - 1, ROWS - 2))[k]
    rows = pl.ds(pl.multiple_of(q * CH, CH), CH)
    t = pltpu.roll(ext, (LANES - chunk * 16) % LANES, 1)
    g0 = jnp.concatenate([fy_row, roll(t, -4)], axis=1)
    part = jnp.concatenate([part_row, roll(t, -10)], axis=1)
    flux = jnp.concatenate([flux_row, roll(t, -14)], axis=1)
    c = sg * 0.25
    eps = c * flux_edge[k, rows, :]
    dh1 = -c * g0
    du1 = -0.25 * ddx(dh1)
    dv_e = -c * (has * (part + eps))
    dv_n = -c * dh1
    h1 = height_edge[k, rows, :] + dh1
    g2 = flux + c * (beyond[2 * k] * h1)
    He, Hn = wide_bath[e], wide_bath[n]
    flow_n = Hn * dv_n
    a = dh1 - 0.25 * (ddx(He * du1) - sg * flow_n + sg * g2)
    b = -c * (He * dv_e)
    d = -c * flow_n
    return eps, du1, dv_e, dv_n, a, b, d


def sums_kernel(
    ntiles, members, scale,
    wide_bath, fy_n, fy_s, msg_n, msg_s, flux_edge, height_edge, seen, index, count, value, sd,
    mine, theirs, beyond, change, sums,
):
    tile = lax.axis_index("lat")
    has = (jnp.where(tile > 0, 1.0, 0.0), jnp.where(tile < ntiles - 1, 1.0, 0.0))
    beyond_rows((msg_n, msg_s), beyond)
    slots = index.shape[1]

    def chunk(q, carry):
        dst = pl.ds(pl.multiple_of(q * CH, CH), CH)
        for k, fy, msg in ((0, fy_n, msg_n), (1, fy_s, msg_s)):
            far = pl.ds(pl.multiple_of(COLS + q * CH, CH), CH)
            ext = msg[pl.ds(pl.multiple_of(EXT + (q // PER) * CH, CH), CH), :LANES]
            new = edge_change(
                k, has[k], q, q % PER, fy[dst, :], msg[dst, :], msg[far, :], ext,
                flux_edge, height_edge, wide_bath, beyond,
            )
            for j in range(3):
                change[3 * k + j, dst, :] = new[4 + j][:, :COLS]
        return carry

    each(members // CH, chunk, 4)(0)
    rows = (0, 1, 2, ROWS - 1, ROWS - 2, ROWS - 3)
    hx = seen[...] + observe(index, [(r, change[j]) for j, r in enumerate(rows)])
    used = jnp.where(lanes_of((1, slots)) < count[0, 0], 1.0, 0.0)
    sigma = sd[...] * scale
    hmean = jnp.mean(hx, axis=0, keepdims=True)
    anom = (hx - hmean) * (used / (math.sqrt(members - 1) * sigma))
    innov = (value[...] - hmean) / sigma * used
    gram = dot(anom, anom, 1, 1)
    proj = dot(jnp.broadcast_to(innov, (8, slots)), anom, 1, 1)
    n = LANES
    ln, sb = lanes_of((n, n)), lax.broadcasted_iota(jnp.int32, (n, n), 0)
    last = gram[n:, n:]
    sums[0:n, :] = jnp.where(ln >= sb, gram[:n, :n], last)
    sums[n : 2 * n, :] = gram[:n, n:]
    sums[2 * n :, :] = jnp.zeros((16, n), jnp.float32)
    sums[2 * n : 2 * n + 1, :] = jnp.sum(jnp.where(ln == sb, last, 0.0), axis=0, keepdims=True)
    sums[2 * n + 1 : 2 * n + 2, :] = proj[0:1, :n]
    sums[2 * n + 2 : 2 * n + 3, :] = proj[0:1, n:]
    part = mine.shape[0]
    core = lax.axis_index("lon") % 2
    mine[...] = sums[pl.ds(pl.multiple_of(core * part, 8), part), :]
    theirs[...] = sums[pl.ds(pl.multiple_of((1 - core) * part, 8), part), :]


def complete_kernel(
    nrows, ntiles, first, wide_bath, beyond, fcor, fy_n, fy_s,
    part_n, flux_n, ext_n, part_s, flux_s, ext_s, flux_edge, height_edge, wind_edge, fields, out,
):
    tile = lax.axis_index("lat")
    base = tile * nrows
    has = (jnp.where(tile > 0, 1.0, 0.0), jnp.where(tile < ntiles - 1, 1.0, 0.0))

    def chunk(q, carry):
        loc = pl.ds(pl.multiple_of(q * CH, CH), CH)
        rows = loc
        there = pl.ds(pl.multiple_of(first + q * CH, CH), CH)
        for k, sg, e, fy, part, flux, ext in (
            (0, -1, 0, fy_n, part_n, flux_n, ext_n),
            (1, 1, ROWS - 1, fy_s, part_s, flux_s, ext_s),
        ):
            eps, du1, dv_e, dv_n, a, b, d = edge_change(
                k, has[k], q, q, fy[loc, :], part[loc, :], flux[loc, :], ext[:, :LANES],
                flux_edge, height_edge, wide_bath, beyond,
            )
            c = sg * 0.25
            flow = wide_bath[e] * dv_e
            flow = flow[:, :COLS] + wide_bath[e][:, :COLS] * wind_edge[k, rows, :]
            bend = ddx(beyond[2 * k] * (-0.25 * ddx(eps))) + 0.25 * (beyond[2 * k + 1] * eps)
            g3 = has[k] * (eps[:, :COLS] - 0.25 * (bend[:, :COLS] - sg * flow))
            cut = lambda x: x[:, :COLS]
            f0, f1 = 0.5 * fcor[base + e], 0.5 * fcor[base + e - sg]
            r = [e - sg * j for j in range(4)]
            upd = (
                (0, r[0], cut(a)),
                (0, r[1], cut(b)),
                (0, r[2], cut(d)),
                (1, r[0], cut(du1 + f0 * dv_e - 0.25 * ddx(a))),
                (1, r[1], cut(f1 * dv_n - 0.25 * ddx(b))),
                (1, r[2], cut(-0.25 * ddx(d))),
                (2, r[0], cut(dv_e - f0 * du1) - c * (g3 - cut(b))),
                (2, r[1], cut(dv_n - c * (a - d))),
                (2, r[2], cut(-c * b)),
                (2, r[3], cut(-c * d)),
            )
            for i, j, x in upd:
                out[i, j, there, :] = fields[i, j, there, :] + x
        return carry

    each(PER, chunk, 4)(0)


def elim(a, dst, base):
    n = LANES
    groups = n // 8
    lane = lanes_of((8, n))
    sub = lax.broadcasted_iota(jnp.int32, (8, n), 0)
    A = [a[8 * g : 8 * g + 8, :] for g in range(groups)]
    X = [(lane == sub + 8 * g).astype(jnp.float32) for g in range(groups)]

    def body(live, it, carry):
        A, X = list(carry[:live]), list(carry[live:])
        cols = [[jnp.broadcast_to(A[g][:, k : k + 1], (8, n)) for k in range(8)] for g in range(live)]
        C, P, Z = cols[0], A[0], X[0]
        rows = Z
        for k in range(8):
            pick = lambda x: jnp.broadcast_to(x[k : k + 1, :], (8, n))
            here = sub == k
            d = pick(C[k])
            inv = 1.0 / d
            rows = jnp.where(here, Z * lax.rsqrt(d), rows)
            ra, rx = pick(P) * inv, pick(Z) * inv
            for j in range(k + 1, 8):
                rc = pick(C[j]) * inv
                C[j] = jnp.where(here, rc, C[j] - C[k] * rc)
            P = jnp.where(here, ra, P - C[k] * ra)
            Z = jnp.where(here, rx, Z - C[k] * rx)
        dst[pl.ds(pl.multiple_of(base + it * 8, 8), 8), :] = rows
        for k in range(8):
            rp, rz = (jnp.broadcast_to(x[k : k + 1, :], (8, n)) for x in (P, Z))
            for g in range(1, live):
                A[g] = A[g] - cols[g][k] * rp
                X[g] = X[g] - cols[g][k] * rz
        z = jnp.zeros((8, n), jnp.float32)
        A = [roll(A[g], -8) for g in range(1, live)] + [z]
        return tuple(A) + tuple(X[1:]) + (z,)

    seg = 4
    for first in range(0, groups, seg):
        live = groups - first
        out = lax.fori_loop(first, first + seg, functools.partial(body, live), tuple(A) + tuple(X))
        A, X = list(out[: live - seg]), list(out[live : 2 * live - seg])


def factor_kernel(members, mine, other, mix, inverse, g_ref):
    n = LANES
    part = mine.shape[0]
    core = lax.axis_index("lon") % 2
    g_ref[pl.ds(pl.multiple_of(core * part, 8), part), :] = mine[...]
    g_ref[pl.ds(pl.multiple_of((1 - core) * part, 8), part), :] = other[...]
    lane, sub = lanes_of((n, n)), lax.broadcasted_iota(jnp.int32, (n, n), 0)
    both = g_ref[0:n, :]
    g12 = g_ref[n : 2 * n, :]
    tail = g_ref[2 * n : 2 * n + 8, :]
    eye = (lane == sub).astype(jnp.float32)
    up = jnp.where(lane >= sub, both, 0.0)
    low = jnp.where(lane < sub, both, 0.0)
    g11 = up + jnp.where(lane > sub, up, 0.0).T + eye
    g22 = low + low.T + jnp.where(lane == sub, jnp.broadcast_to(tail[0:1, :], (n, n)), 0.0) + eye
    elim(g11, inverse, 0)
    x11 = inverse[0:n, :]
    y12 = dot(x11, g12, 1, 0)
    elim(g22 - dot(y12, y12, 0, 0), inverse, n)
    x22 = inverse[n : 2 * n, :]
    x21 = -dot(x22, dot(y12, x11, 0, 0), 1, 0)
    p1 = jnp.broadcast_to(tail[1:2, :], (8, n))
    p2 = jnp.broadcast_to(tail[2:3, :], (8, n))
    q1 = dot(p1, x11, 1, 1)
    q2 = dot(p1, x21, 1, 1) + dot(p2, x22, 1, 1)
    c = 1.0 / math.sqrt(members - 1)
    w1 = (dot(q1, x11, 1, 0) + dot(q2, x21, 1, 0))[0:1, :] * c
    w2 = dot(q2, x22, 1, 0)[0:1, :] * c
    ws = jnp.sum(w1, axis=1, keepdims=True) + jnp.sum(w2, axis=1, keepdims=True)
    r = 1.0 / members
    s1 = (1.0 - ws - jnp.sum(x11, axis=1, keepdims=True)) * r
    s2 = (1.0 - ws - jnp.sum(x21, axis=1, keepdims=True) - jnp.sum(x22, axis=1, keepdims=True)) * r
    mix[0:n, 0:n] = x11 + (w1 + s1)
    mix[0:n, n:] = w2 + s1
    mix[n:, 0:n] = x21 + (w1 + s2)
    mix[n:, n:] = x22 + (w2 + s2)


def apply_kernel(mix, fields, late_n, late_s, out):
    high, low = split(mix[...], 2)
    wind = jnp.where(pl.program_id(0) == 2, 0.25, 0.0)
    for i in range(ROWS):
        x = fields[0, i]
        if i == 0:
            x = x + wind * late_n[...]
        if i == ROWS - 1:
            x = x - wind * late_s[...]
        a, b = split(x, 2)
        res = bdot(high, a) + (bdot(high, b) + bdot(low, a))
        out[0, pl.ds(i, x.shape[0], stride=ROWS), :] = res


def whole(shape):
    return pl.BlockSpec(shape, lambda *_: (0,) * len(shape))


def f32(*shape):
    return jax.ShapeDtypeStruct(shape, jnp.float32)


def flips(n, bit):
    return [(i, i ^ bit) for i in range(n)]


def bits(n):
    return [1 << k for k in range(n.bit_length() - 1)]


def total(mine, theirs, late_n, late_s, south, north):
    nlon, nlat = lax.axis_size("lon"), lax.axis_size("lat")
    y = mine + lax.ppermute(theirs, "lon", flips(nlon, 1))
    lon, lat = bits(nlon), bits(nlat)
    stages = [("lat", nlat, lat[:1]), ("lon", nlon, lon[1:3]), ("lon", nlon, lon[3:]), ("lat", nlat, lat[1:])]
    late = []
    for k, (axis, n, todo) in enumerate(stages):
        hops = todo if len(todo) == 1 else [todo[0], todo[1], todo[0] | todo[1]]
        if k == 2:
            y, late_s = lax.optimization_barrier((y, late_s))
            late.append(lax.ppermute(late_s, "lat", south))
        if k == 3:
            y, late_n = lax.optimization_barrier((y, late_n))
            late.append(lax.ppermute(late_n, "lat", north))
        parts = [lax.ppermute(y, axis, flips(n, b)) for b in hops]
        for p in parts:
            y = y + p
    other = lax.ppermute(y, "lon", flips(nlon, 1))
    return y, other, late


def body(state, bathymetry, obs_index, obs_count, obs_value, obs_sd):
    members = state.shape[1]
    nlat, nlon = lax.axis_size("lat"), lax.axis_size("lon")
    slots = obs_index.shape[2]
    total_rows = ROWS * nlat
    fcor = np.sin(math.pi / 3.0 * ((np.arange(total_rows) + 0.5) / total_rows - 0.5)).astype(np.float32)
    flat = pltpu.with_memory_space_constraint(state.reshape(3, members * ROWS, COLS), pltpu.HBM)
    blk = CH * PER
    grid = (members // blk,)
    state_specs = [
        pl.BlockSpec((3, blk * ROWS, LANES), lambda s: (0, s, 0)),
        pl.BlockSpec((3, blk * ROWS, LANES), lambda s: (0, s, 1)),
    ]
    thin = pl.BlockSpec((blk, LANES), lambda s: (s, 0))
    row = pl.BlockSpec((blk, COLS), lambda s: (s, 0))
    bath_spec = whole((ROWS, COLS))
    smem = pl.BlockSpec(memory_space=pltpu.SMEM)

    wide_bath_shape = (ROWS, CH, WIDE)
    east = [(i, (i + 1) % nlon) for i in range(nlon)]
    west = [(j, i) for i, j in east]
    south = [(i, i + 1) for i in range(nlat - 1)]
    north = [(j, i) for i, j in south]

    to_east, to_west = pl.pallas_call(
        edges_kernel,
        grid=grid,
        in_specs=state_specs + [bath_spec],
        out_specs=[thin, thin],
        out_shape=[f32(members, LANES)] * 2,
        compiler_params=clip(24),
        name="edges",
    )(flat, flat, bathymetry)
    from_west = lax.ppermute(to_east, "lon", east)
    from_east = lax.ppermute(to_west, "lon", west)

    wind_specs = [
        pl.BlockSpec((1, blk * ROWS, LANES), lambda s: (2, s, 0)),
        pl.BlockSpec((1, blk * ROWS, LANES), lambda s: (2, s, 1)),
    ]
    to_north, to_south = pl.pallas_call(
        flux_kernel,
        grid=grid,
        in_specs=wind_specs + [bath_spec],
        out_specs=[row, row],
        out_shape=[f32(members, COLS)] * 2,
        compiler_params=clip(24),
        name="flux",
    )(flat, flat, bathymetry)
    fy_n = lax.ppermute(to_south, "lat", south)
    fy_s = lax.ppermute(to_north, "lat", north)

    msg_n, msg_s, wide_bath = pl.pallas_call(
        functools.partial(border_kernel, ROWS),
        grid=grid,
        in_specs=state_specs + [bath_spec, thin, thin, smem],
        out_specs=[whole((MSG, COLS))] * 2 + [whole(wide_bath_shape)],
        out_shape=[f32(MSG, COLS)] * 2 + [f32(*wide_bath_shape)],
        compiler_params=clip(24),
        name="border",
    )(flat, flat, bathymetry, from_east, from_west, fcor)
    got_n = lax.ppermute(msg_s, "lat", south)
    got_s = lax.ppermute(msg_n, "lat", north)

    one = lambda x: x.reshape(1, slots)
    obs = whole((1, slots))
    edge = whole((2, members, WIDE))
    blocks = members // blk
    wb_spec, bey_spec = whole(wide_bath_shape), whole((4, CH, WIDE))
    fields_shape = VM((3, ROWS, members, COLS), jnp.float32)
    fields, flux_edge, height_edge, wind_edge, seen, late_n, late_s = pl.pallas_call(
        functools.partial(local_kernel, ROWS),
        grid=grid,
        in_specs=state_specs + [wb_spec, thin, thin, smem, obs],
        out_specs=[
            pl.BlockSpec((3, ROWS, blk, COLS), lambda s: (0, 0, s, 0)),
            pl.BlockSpec((2, blk, WIDE), lambda s: (0, s, 0)),
            pl.BlockSpec((2, blk, WIDE), lambda s: (0, s, 0)),
            pl.BlockSpec((2, blk, COLS), lambda s: (0, s, 0)),
            whole((members, slots)),
            row,
            row,
        ],
        out_shape=[
            fields_shape, f32(2, members, WIDE), f32(2, members, WIDE),
            f32(2, members, COLS), f32(members, slots), f32(members, COLS), f32(members, COLS),
        ],
        scratch_shapes=[VM((ROWS, members, COLS), jnp.float32)],
        compiler_params=clip(24),
        name="local",
    )(flat, flat, wide_bath, from_east, from_west, fcor, one(obs_index))

    part = f32(136, LANES)
    mine, theirs, beyond = pl.pallas_call(
        functools.partial(sums_kernel, nlat, members, math.sqrt(slots * nlat * nlon) / 16.0),
        grid=(1,),
        in_specs=[wb_spec]
        + [whole((members, COLS))] * 2
        + [whole((MSG, COLS))] * 2
        + [edge, edge, whole((members, slots)), obs, smem, obs, obs],
        out_specs=[whole(part.shape), whole(part.shape), bey_spec],
        out_shape=[part, part, f32(4, CH, WIDE)],
        scratch_shapes=[VM((6, members, COLS), jnp.float32), VM((272, LANES), jnp.float32)],
        compiler_params=clip(24),
        name="sums",
    )(
        wide_bath, fy_n, fy_s, got_n, got_s, flux_edge, height_edge, seen,
        one(obs_index), obs_count, one(obs_value), one(obs_sd),
    )

    for k in range(blocks):
        at = lambda rows, j: pl.BlockSpec((rows, COLS), lambda s: (j, 0))
        msg_specs = [at(blk, k), at(blk, COLS // blk + k), at(CH, EXT // CH + k)]
        edge_k = pl.BlockSpec((2, blk, WIDE), lambda s, k=k: (0, k, 0))
        wind_k = pl.BlockSpec((2, blk, COLS), lambda s, k=k: (0, k, 0))
        here = pl.BlockSpec(memory_space=VM)
        fields = pl.pallas_call(
            functools.partial(complete_kernel, ROWS, nlat, k * blk),
            grid=(1,),
            in_specs=[wb_spec, bey_spec, smem, at(blk, k), at(blk, k)]
            + msg_specs * 2
            + [edge_k, edge_k, wind_k, here],
            out_specs=here,
            out_shape=fields_shape,
            input_output_aliases={14: 0},
            compiler_params=clip(24),
            name="complete",
        )(
            wide_bath, beyond, fcor, fy_n, fy_s, got_n, got_n, got_n, got_s, got_s, got_s,
            flux_edge, height_edge, wind_edge, fields,
        )

    sum_mine, sum_other, late = total(mine, theirs, late_n, late_s, south, north)
    fields = pltpu.with_memory_space_constraint(fields, pltpu.VMEM)

    mix = pl.pallas_call(
        functools.partial(factor_kernel, members),
        out_shape=f32(members, members),
        in_specs=[pl.BlockSpec(memory_space=VM)] * 2,
        out_specs=pl.BlockSpec(memory_space=VM),
        scratch_shapes=[VM((members, LANES), jnp.float32), VM((272, LANES), jnp.float32)],
        compiler_params=clip(8),
        name="factor",
    )(sum_mine, sum_other)

    half = pl.BlockSpec((members, LANES), lambda c, j: (0, j))
    analysis = pl.pallas_call(
        apply_kernel,
        grid=(3, COLS // LANES),
        in_specs=[
            whole((members, members)),
            pl.BlockSpec((1, ROWS, members, LANES), lambda c, j: (c, 0, 0, j)),
            half,
            half,
        ],
        out_specs=pl.BlockSpec((1, members * ROWS, LANES), lambda c, j: (c, 0, j)),
        out_shape=f32(3, members * ROWS, COLS),
        compiler_params=clip(24),
        name="mix",
    )(mix, fields, *late)
    return analysis.reshape(state.shape)


def solution(mesh):
    return jax.shard_map(
        body,
        mesh=mesh,
        in_specs=(
            P(None, None, "lat", "lon"),
            P("lat", "lon"),
            P("lat", "lon", None),
            P("lat", "lon"),
            P("lat", "lon", None),
            P("lat", "lon", None),
        ),
        out_specs=P(None, None, "lat", "lon"),
        check_vma=False,
    )
```

```python
import functools
import math

import jax
import jax.numpy as jnp
import numpy as np
from jax import lax
from jax.experimental import pallas as pl
from jax.experimental.pallas import tpu as pltpu
from jax.sharding import PartitionSpec as P


HI = lax.Precision.HIGHEST
CH = 8
PER = 8
ROWS = 8
COLS = 256
WIDE = 384
LANES = 128
EXT = 2 * COLS
BATH = EXT + 16
MSG = BATH + 8
VM = pltpu.VMEM


def each(trips, fn, together):
    def turn(t, carry):
        for j in range(together):
            carry = fn(t * together + j, carry)
        return carry

    return lambda init: lax.fori_loop(0, trips // together, turn, init)


def roll(x, shift):
    return pltpu.roll(x, shift % x.shape[1], 1)


def ddx(x):
    return roll(x, -1) - roll(x, 1)


def ext_at(block, row):
    half = pl.ds(pl.multiple_of((block % 2) * LANES, LANES), LANES)
    return pl.ds(pl.multiple_of(row + (block // 2) * CH, CH), CH), half


def lanes_of(shape):
    return lax.broadcasted_iota(jnp.int32, shape, 1)


def field_rows(lo, hi, c, q, i):
    rows = pl.ds(q * (CH * ROWS) + i, CH, stride=ROWS)
    return lo[c, rows, :], hi[c, rows, :]


def flux_kernel(lo, hi, bath, to_north, to_south):
    def chunk(q, carry):
        out = pl.ds(pl.multiple_of(q * CH, CH), CH)
        for i, ref in ((0, to_north), (ROWS - 1, to_south)):
            a, b = field_rows(lo, hi, 0, q, i)
            ref[out, :LANES] = a * bath[i : i + 1, :LANES]
            ref[out, LANES:] = b * bath[i : i + 1, LANES:]
        return carry

    each(PER, chunk, 4)(0)


def edges_kernel(lo, hi, bath, to_east, to_west):
    lane = lanes_of((CH, LANES))
    first = jnp.zeros((CH, LANES), jnp.float32)
    last = jnp.zeros((CH, LANES), jnp.float32)
    place = lambda spot: (lane >= spot) & (lane < spot + 4)
    for i in range(ROWS):
        spot = 4 * (3 * ROWS + i)
        a = jnp.broadcast_to(bath[i : i + 1, :LANES], (CH, LANES))
        b = jnp.broadcast_to(bath[i : i + 1, LANES:], (CH, LANES))
        first = jnp.where(place(spot), roll(a, spot), first)
        last = jnp.where(place(spot), roll(b, spot + 4), last)

    def chunk(q, carry):
        west, east = first, last
        out = pl.ds(pl.multiple_of(q * CH, CH), CH)
        for c in range(3):
            for i in range(ROWS):
                a, b = field_rows(lo, hi, c, q, i)
                spot = 4 * (c * ROWS + i)
                west = jnp.where(place(spot), roll(a, spot), west)
                east = jnp.where(place(spot), roll(b, spot + 4), east)
        to_east[out, :] = east
        to_west[out, :] = west
        return carry

    each(PER, chunk, 2)(0)


def bath_rows(bath, from_east, from_west, wide_bath):
    lane = lanes_of((CH, LANES))
    e, w = from_east[0:CH, :], from_west[0:CH, :]
    for i in range(ROWS):
        spot = 4 * (3 * ROWS + i)
        tail = jnp.where(lane < 4, roll(e, -spot), roll(w, 124 - spot))
        wide_bath[i, :, :COLS] = jnp.broadcast_to(bath[i : i + 1, :], (CH, COLS))
        wide_bath[i, :, COLS:] = tail


def wide_rows(lo, hi, e, w, lane, q, c, i):
    a, b = field_rows(lo, hi, c, q, i)
    spot = 4 * (c * ROWS + i)
    tail = jnp.where(lane < 4, roll(e, -spot), roll(w, 124 - spot))
    return jnp.concatenate([a, b, tail], axis=1)


def border_kernel(nrows, lo, hi, bath, from_east, from_west, fcor, msg_n, msg_s, wide_bath):
    step = pl.program_id(0)
    base = lax.axis_index("lat") * nrows

    @pl.when(step == 0)
    def _():
        bath_rows(bath, from_east, from_west, wide_bath)
        for msg, r0, r1 in ((msg_n, 0, 1), (msg_s, ROWS - 1, ROWS - 2)):
            msg[EXT:MSG, :] = jnp.zeros((MSG - EXT, COLS), jnp.float32)
            msg[BATH : BATH + 1, :] = bath[r0 : r0 + 1, :]
            msg[BATH + 1 : BATH + 2, :] = bath[r1 : r1 + 1, :]
            msg[BATH + 2 : BATH + 3, :LANES] = wide_bath[r0, 0:1, COLS:]

    lane = lanes_of((CH, LANES))

    def chunk(q, carry):
        out = pl.ds(pl.multiple_of(q * CH, CH), CH)
        dst = pl.ds(pl.multiple_of(step * (CH * PER) + q * CH, CH), CH)
        dst_q = pl.ds(pl.multiple_of(COLS + step * (CH * PER) + q * CH, CH), CH)
        e, w = from_east[out, :], from_west[out, :]
        new = []
        for msg, first, sg, ext in ((msg_n, 0, 1, carry[0]), (msg_s, ROWS - 1, -1, carry[1])):
            rows = [first + sg * k for k in range(3)]
            H = [wide_bath[r] for r in rows]
            load = lambda c, k: wide_rows(lo, hi, e, w, lane, q, c, rows[k])
            h = [load(0, k) for k in range(2)]
            u = [load(1, k) for k in range(2)]
            v = [load(2, k) for k in range(3)]
            f0 = fcor[base + rows[0]]
            fy = [H[k] * v[k] for k in range(3)]
            dfx = [ddx(H[k] * u[k]) for k in range(2)]
            h1a = h[1] - 0.25 * (dfx[1] + sg * (fy[2] - fy[0]))
            part = h[0] - 0.25 * (dfx[0] + sg * fy[1])
            flux = H[0] * (v[0] - (0.5 * f0) * u[0] - (sg * 0.25) * h1a)
            msg[dst, :] = part[:, :COLS]
            msg[dst_q, :] = flux[:, :COLS]
            t = jnp.where(
                lane < 8,
                roll(fy[0][:, COLS:], 4),
                jnp.where(lane < 12, roll(part[:, COLS:], 10), roll(flux[:, COLS:], 14)),
            )
            t = pltpu.roll(t, q * 16, 1)
            new.append(jnp.where(lane // 16 == q, t, ext))
        return tuple(new)

    zero = jnp.zeros((CH, LANES), jnp.float32)
    exts = each(PER, chunk, 4)((zero, zero))
    for msg, ext in ((msg_n, exts[0]), (msg_s, exts[1])):
        msg[ext_at(step, EXT)] = ext


def split(x, pieces):
    parts = []
    for k in range(pieces):
        p = x.astype(jnp.bfloat16)
        parts.append(p)
        if k + 1 < pieces:
            x = x - p.astype(jnp.float32)
    return parts


def dot(a, b, ca, cb):
    return lax.dot_general(
        a, b, (((ca,), (cb,)), ((), ())), precision=HI, preferred_element_type=jnp.float32
    )


def bdot(a, b):
    return jnp.dot(a, b, preferred_element_type=jnp.float32)


def clip(limit):
    return pltpu.CompilerParams(vmem_limit_bytes=limit << 20)


def local_kernel(
    nrows, lo, hi, wide_bath, from_east, from_west, fcor, index,
    out, flux_edge, height_edge, wind_edge, seen, late_n, late_s, height,
):
    step = pl.program_id(0)
    base = lax.axis_index("lat") * nrows
    lane = lanes_of((CH, LANES))

    def across(y, i):
        if i == 0:
            return y[1]
        if i == ROWS - 1:
            return -y[i - 1]
        return y[i + 1] - y[i - 1]

    def chunk(q, carry):
        loc = pl.ds(pl.multiple_of(q * CH, CH), CH)
        dst = pl.ds(pl.multiple_of(step * (CH * PER) + q * CH, CH), CH)
        e, w = from_east[loc, :], from_west[loc, :]
        load = lambda c, i: wide_rows(lo, hi, e, w, lane, q, c, i)
        H = [wide_bath[i] for i in range(ROWS)]
        f = [fcor[base + i] for i in range(ROWS)]
        h = [load(0, i) for i in range(ROWS)]
        u = [load(1, i) for i in range(ROWS)]
        v = [load(2, i) for i in range(ROWS)]
        fy = [H[i] * v[i] for i in range(ROWS)]
        h1 = [h[i] - 0.25 * (ddx(H[i] * u[i]) + across(fy, i)) for i in range(ROWS)]
        u1 = [u[i] + (0.5 * f[i]) * v[i] - 0.25 * ddx(h1[i]) for i in range(ROWS)]
        v1 = [v[i] - (0.5 * f[i]) * u[i] - 0.25 * across(h1, i) for i in range(ROWS)]
        for k, i in ((0, 0), (1, ROWS - 1)):
            flux_edge[k, loc, :] = fy[i]
            height_edge[k, loc, :] = h1[i]
            wind_edge[k, loc, :] = v1[i][:, :COLS]
        fy = [H[i] * v1[i] for i in range(ROWS)]
        h2 = [h1[i] - 0.25 * (ddx(H[i] * u1[i]) + across(fy, i)) for i in range(ROWS)]
        for i in range(ROWS):
            u2 = u1[i] + (0.5 * f[i]) * v1[i] - 0.25 * ddx(h2[i])
            v2 = v1[i] - (0.5 * f[i]) * u1[i] - 0.25 * across(h2, i)
            out[0, i, loc, :] = h2[i][:, :COLS]
            out[1, i, loc, :] = u2[:, :COLS]
            out[2, i, loc, :] = v2[:, :COLS]
            height[i, dst, :] = h2[i][:, :COLS]
        late_n[loc, :] = h2[0][:, :COLS]
        late_s[loc, :] = h2[-1][:, :COLS]
        return carry

    lax.fori_loop(0, PER, chunk, 0)

    @pl.when(step == pl.num_programs(0) - 1)
    def _():
        seen[...] = observe(index, [(i, height[i]) for i in range(ROWS)], 3)


def observe(index, planes, count):
    slots = index.shape[1]
    sub = lax.broadcasted_iota(jnp.int32, (COLS, slots), 0)
    cell = jnp.broadcast_to(index[...], (COLS, slots))
    left, right = [], []
    for i, plane in planes:
        pick = jnp.where(sub + i * COLS == cell, 1.0, 0.0).astype(jnp.bfloat16)
        left += split(plane, count)
        right += [pick] * count
    return bdot(jnp.concatenate(left, axis=1), jnp.concatenate(right, axis=0))


def beyond_rows(msgs, beyond):
    for k, msg in enumerate(msgs):
        beyond[2 * k, :, :COLS] = jnp.broadcast_to(msg[BATH : BATH + 1, :], (CH, COLS))
        beyond[2 * k, :, COLS:] = jnp.broadcast_to(msg[BATH + 2 : BATH + 3, :LANES], (CH, LANES))
        beyond[2 * k + 1, :, :COLS] = jnp.broadcast_to(msg[BATH + 1 : BATH + 2, :], (CH, COLS))
        beyond[2 * k + 1, :, COLS:] = jnp.zeros((CH, LANES), jnp.float32)


def edge_change(k, has, q, chunk, fy_row, part_row, flux_row, ext, flux_edge, height_edge, wide_bath, beyond):
    sg, e, n = ((-1, 0, 1), (1, ROWS - 1, ROWS - 2))[k]
    rows = pl.ds(pl.multiple_of(q * CH, CH), CH)
    t = pltpu.roll(ext, (LANES - chunk * 16) % LANES, 1)
    g0 = jnp.concatenate([fy_row, roll(t, -4)], axis=1)
    part = jnp.concatenate([part_row, roll(t, -10)], axis=1)
    flux = jnp.concatenate([flux_row, roll(t, -14)], axis=1)
    c = sg * 0.25
    eps = c * flux_edge[k, rows, :]
    dh1 = -c * g0
    du1 = -0.25 * ddx(dh1)
    dv_e = -c * (has * (part + eps))
    dv_n = -c * dh1
    h1 = height_edge[k, rows, :] + dh1
    g2 = flux + c * (beyond[2 * k] * h1)
    He, Hn = wide_bath[e], wide_bath[n]
    flow_n = Hn * dv_n
    a = dh1 - 0.25 * (ddx(He * du1) - sg * flow_n + sg * g2)
    b = -c * (He * dv_e)
    d = -c * flow_n
    return eps, du1, dv_e, dv_n, a, b, d


def sums_kernel(
    ntiles, members, scale,
    wide_bath, fy_n, fy_s, msg_n, msg_s, flux_edge, height_edge, seen, index, count, value, sd,
    mine, theirs, beyond, change, sums,
):
    tile = lax.axis_index("lat")
    has = (jnp.where(tile > 0, 1.0, 0.0), jnp.where(tile < ntiles - 1, 1.0, 0.0))
    beyond_rows((msg_n, msg_s), beyond)
    slots = index.shape[1]

    def chunk(q, carry):
        dst = pl.ds(pl.multiple_of(q * CH, CH), CH)
        for k, fy, msg in ((0, fy_n, msg_n), (1, fy_s, msg_s)):
            far = pl.ds(pl.multiple_of(COLS + q * CH, CH), CH)
            ext = msg[ext_at(q // PER, EXT)]
            new = edge_change(
                k, has[k], q, q % PER, fy[dst, :], msg[dst, :], msg[far, :], ext,
                flux_edge, height_edge, wide_bath, beyond,
            )
            for j in range(3):
                change[3 * k + j, dst, :] = new[4 + j][:, :COLS]
        return carry

    each(members // CH, chunk, 4)(0)
    rows = (0, 1, 2, ROWS - 1, ROWS - 2, ROWS - 3)
    hx = seen[...] + observe(index, [(r, change[j]) for j, r in enumerate(rows)], 2)
    used = jnp.where(lanes_of((1, slots)) < count[0, 0], 1.0, 0.0)
    sigma = sd[...] * scale
    hmean = jnp.mean(hx, axis=0, keepdims=True)
    anom = (hx - hmean) * (used / (math.sqrt(members - 1) * sigma))
    innov = (value[...] - hmean) / sigma * used
    gram = dot(anom, anom, 1, 1)
    proj = dot(jnp.broadcast_to(innov, (8, slots)), anom, 1, 1)
    n = LANES
    ln, sb = lanes_of((n, n)), lax.broadcasted_iota(jnp.int32, (n, n), 0)
    last = gram[n:, n:]
    sums[0:n, :] = jnp.where(ln >= sb, gram[:n, :n], last)
    sums[n : 2 * n, :] = gram[:n, n:]
    sums[2 * n :, :] = jnp.zeros((16, n), jnp.float32)
    sums[2 * n : 2 * n + 1, :] = jnp.sum(jnp.where(ln == sb, last, 0.0), axis=0, keepdims=True)
    sums[2 * n + 1 : 2 * n + 2, :] = proj[0:1, :n]
    sums[2 * n + 2 : 2 * n + 3, :] = proj[0:1, n:]
    part = mine.shape[0]
    core = lax.axis_index("lon") % 2
    mine[...] = sums[pl.ds(pl.multiple_of(core * part, 8), part), :]
    theirs[...] = sums[pl.ds(pl.multiple_of((1 - core) * part, 8), part), :]


def complete_kernel(
    nrows, ntiles, first, wide_bath, beyond, fcor, fy_n, fy_s,
    part_n, flux_n, ext_n, part_s, flux_s, ext_s, flux_edge, height_edge, wind_edge, fields, out,
):
    tile = lax.axis_index("lat")
    base = tile * nrows
    has = (jnp.where(tile > 0, 1.0, 0.0), jnp.where(tile < ntiles - 1, 1.0, 0.0))

    def chunk(q, carry):
        loc = pl.ds(pl.multiple_of(q * CH, CH), CH)
        rows = loc
        full = first // CH + q
        there = pl.ds(pl.multiple_of(first + q * CH, CH), CH)
        for k, sg, e, fy, part, flux, ext in (
            (0, -1, 0, fy_n, part_n, flux_n, ext_n),
            (1, 1, ROWS - 1, fy_s, part_s, flux_s, ext_s),
        ):
            eps, du1, dv_e, dv_n, a, b, d = edge_change(
                k, has[k], q, full % PER, fy[loc, :], part[loc, :], flux[loc, :], ext[ext_at((full // PER) % 2, 0)],
                flux_edge, height_edge, wide_bath, beyond,
            )
            c = sg * 0.25
            flow = wide_bath[e] * dv_e
            flow = flow[:, :COLS] + wide_bath[e][:, :COLS] * wind_edge[k, rows, :]
            bend = ddx(beyond[2 * k] * (-0.25 * ddx(eps))) + 0.25 * (beyond[2 * k + 1] * eps)
            g3 = has[k] * (eps[:, :COLS] - 0.25 * (bend[:, :COLS] - sg * flow))
            cut = lambda x: x[:, :COLS]
            f0, f1 = 0.5 * fcor[base + e], 0.5 * fcor[base + e - sg]
            r = [e - sg * j for j in range(4)]
            upd = (
                (0, r[0], cut(a)),
                (0, r[1], cut(b)),
                (0, r[2], cut(d)),
                (1, r[0], cut(du1 + f0 * dv_e - 0.25 * ddx(a))),
                (1, r[1], cut(f1 * dv_n - 0.25 * ddx(b))),
                (1, r[2], cut(-0.25 * ddx(d))),
                (2, r[0], cut(dv_e - f0 * du1) - c * (g3 - cut(b))),
                (2, r[1], cut(dv_n - c * (a - d))),
                (2, r[2], cut(-c * b)),
                (2, r[3], cut(-c * d)),
            )
            for i, j, x in upd:
                out[i, j, there, :] = fields[i, j, there, :] + x
        return carry

    trips = fy_n.shape[0] // CH
    each(trips, chunk, min(4, trips))(0)


def elim(a, dst, base):
    n = LANES
    groups = n // 8
    lane = lanes_of((8, n))
    sub = lax.broadcasted_iota(jnp.int32, (8, n), 0)
    A = [a[8 * g : 8 * g + 8, :] for g in range(groups)]
    X = [(lane == sub + 8 * g).astype(jnp.float32) for g in range(groups)]

    def body(live, it, carry):
        A, X = list(carry[:live]), list(carry[live:])
        column = lambda g, k: jnp.broadcast_to(A[g][:, k : k + 1], (8, n))
        C, P, Z = [column(0, k) for k in range(8)], A[0], X[0]
        rows = Z
        for k in range(8):
            pick = lambda x: jnp.broadcast_to(x[k : k + 1, :], (8, n))
            here = sub == k
            d = pick(C[k])
            inv = 1.0 / d
            rows = jnp.where(here, Z * lax.rsqrt(d), rows)
            ra, rx = pick(P) * inv, pick(Z) * inv
            for j in range(k + 1, 8):
                rc = pick(C[j]) * inv
                C[j] = jnp.where(here, rc, C[j] - C[k] * rc)
            P = jnp.where(here, ra, P - C[k] * ra)
            Z = jnp.where(here, rx, Z - C[k] * rx)
        dst[pl.ds(pl.multiple_of(base + it * 8, 8), 8), :] = rows
        spread = lambda x: [jnp.broadcast_to(x[k : k + 1, :], (8, n)) for k in range(8)]
        rp, rz = spread(P), spread(Z)
        for g in range(1, live):
            cols = [column(g, k) for k in range(8)]
            for k in range(8):
                A[g] = A[g] - cols[k] * rp[k]
                X[g] = X[g] - cols[k] * rz[k]
        z = jnp.zeros((8, n), jnp.float32)
        A = [roll(A[g], -8) for g in range(1, live)] + [z]
        return tuple(A) + tuple(X[1:]) + (z,)

    seg = 2
    for first in range(0, groups, seg):
        live = groups - first
        out = lax.fori_loop(first, first + seg, functools.partial(body, live), tuple(A) + tuple(X))
        A, X = list(out[: live - seg]), list(out[live : 2 * live - seg])


def factor_kernel(members, mine, other, mix, inverse, g_ref):
    n = LANES
    part = mine.shape[0]
    core = lax.axis_index("lon") % 2
    g_ref[pl.ds(pl.multiple_of(core * part, 8), part), :] = mine[...]
    g_ref[pl.ds(pl.multiple_of((1 - core) * part, 8), part), :] = other[...]
    lane, sub = lanes_of((n, n)), lax.broadcasted_iota(jnp.int32, (n, n), 0)
    both = g_ref[0:n, :]
    g12 = g_ref[n : 2 * n, :]
    tail = g_ref[2 * n : 2 * n + 8, :]
    eye = (lane == sub).astype(jnp.float32)
    up = jnp.where(lane >= sub, both, 0.0)
    low = jnp.where(lane < sub, both, 0.0)
    g11 = up + jnp.where(lane > sub, up, 0.0).T + eye
    g22 = low + low.T + jnp.where(lane == sub, jnp.broadcast_to(tail[0:1, :], (n, n)), 0.0) + eye
    elim(g11, inverse, 0)
    x11 = inverse[0:n, :]
    y12 = dot(x11, g12, 1, 0)
    elim(g22 - dot(y12, y12, 0, 0), inverse, n)
    x22 = inverse[n : 2 * n, :]
    x21 = -dot(x22, dot(y12, x11, 0, 0), 1, 0)
    p1 = jnp.broadcast_to(tail[1:2, :], (8, n))
    p2 = jnp.broadcast_to(tail[2:3, :], (8, n))
    q1 = dot(p1, x11, 1, 1)
    q2 = dot(p1, x21, 1, 1) + dot(p2, x22, 1, 1)
    c = 1.0 / math.sqrt(members - 1)
    w1 = (dot(q1, x11, 1, 0) + dot(q2, x21, 1, 0))[0:1, :] * c
    w2 = dot(q2, x22, 1, 0)[0:1, :] * c
    ws = jnp.sum(w1, axis=1, keepdims=True) + jnp.sum(w2, axis=1, keepdims=True)
    r = 1.0 / members
    s1 = (1.0 - ws - jnp.sum(x11, axis=1, keepdims=True)) * r
    s2 = (1.0 - ws - jnp.sum(x21, axis=1, keepdims=True) - jnp.sum(x22, axis=1, keepdims=True)) * r
    mix[0:n, 0:n] = x11 + (w1 + s1)
    mix[0:n, n:] = w2 + s1
    mix[n:, 0:n] = x21 + (w1 + s2)
    mix[n:, n:] = x22 + (w2 + s2)


def apply_kernel(mix, fields, late_n, late_s, out, left):
    members = mix.shape[0]

    @pl.when((pl.program_id(0) == 0) & (pl.program_id(1) == 0))
    def _():
        high, low = split(mix[...], 2)
        left[:, :members] = high
        left[:, members : 2 * members] = high
        left[:, 2 * members :] = low

    wind = jnp.where(pl.program_id(0) == 2, 0.25, 0.0)
    for i in range(ROWS):
        x = fields[0, i]
        if i == 0:
            x = x + wind * late_n[...]
        if i == ROWS - 1:
            x = x - wind * late_s[...]
        a, b = split(x, 2)
        out[0, pl.ds(i, members, stride=ROWS), :] = bdot(left[...], jnp.concatenate([a, b, a], axis=0))


def whole(shape):
    return pl.BlockSpec(shape, lambda *_: (0,) * len(shape))


def f32(*shape):
    return jax.ShapeDtypeStruct(shape, jnp.float32)


def flips(n, bit):
    return [(i, i ^ bit) for i in range(n)]


def bits(n):
    return [1 << k for k in range(n.bit_length() - 1)]


def total(mine, theirs, late_n, late_s, south, north):
    nlon, nlat = lax.axis_size("lon"), lax.axis_size("lat")
    y = mine + lax.ppermute(theirs, "lon", flips(nlon, 1))
    lon, lat = bits(nlon), bits(nlat)
    stages = [("lat", nlat, lat[:1]), ("lon", nlon, lon[1:3]), ("lon", nlon, lon[3:]), ("lat", nlat, lat[1:])]
    late = []
    for k, (axis, n, todo) in enumerate(stages):
        hops = todo if len(todo) == 1 else [todo[0], todo[1], todo[0] | todo[1]]
        if k == 2:
            y, late_s = lax.optimization_barrier((y, late_s))
            late.append(lax.ppermute(late_s, "lat", south))
        if k == 3:
            y, late_n = lax.optimization_barrier((y, late_n))
            late.append(lax.ppermute(late_n, "lat", north))
        parts = [lax.ppermute(y, axis, flips(n, b)) for b in hops]
        for p in parts:
            y = y + p
    other = lax.ppermute(y, "lon", flips(nlon, 1))
    return y, other, late


def body(state, bathymetry, obs_index, obs_count, obs_value, obs_sd):
    members = state.shape[1]
    nlat, nlon = lax.axis_size("lat"), lax.axis_size("lon")
    slots = obs_index.shape[2]
    total_rows = ROWS * nlat
    fcor = np.sin(math.pi / 3.0 * ((np.arange(total_rows) + 0.5) / total_rows - 0.5)).astype(np.float32)
    flat = pltpu.with_memory_space_constraint(state.reshape(3, members * ROWS, COLS), pltpu.HBM)
    blk = CH * PER
    grid = (members // blk,)
    state_specs = [
        pl.BlockSpec((3, blk * ROWS, LANES), lambda s: (0, s, 0)),
        pl.BlockSpec((3, blk * ROWS, LANES), lambda s: (0, s, 1)),
    ]
    thin = pl.BlockSpec((blk, LANES), lambda s: (s, 0))
    row = pl.BlockSpec((blk, COLS), lambda s: (s, 0))
    bath_spec = whole((ROWS, COLS))
    smem = pl.BlockSpec(memory_space=pltpu.SMEM)

    wide_bath_shape = (ROWS, CH, WIDE)
    east = [(i, (i + 1) % nlon) for i in range(nlon)]
    west = [(j, i) for i, j in east]
    south = [(i, i + 1) for i in range(nlat - 1)]
    north = [(j, i) for i, j in south]

    to_east, to_west = pl.pallas_call(
        edges_kernel,
        grid=grid,
        in_specs=state_specs + [bath_spec],
        out_specs=[thin, thin],
        out_shape=[f32(members, LANES)] * 2,
        compiler_params=clip(24),
        name="edges",
    )(flat, flat, bathymetry)
    from_west = lax.ppermute(to_east, "lon", east)
    from_east = lax.ppermute(to_west, "lon", west)

    wind_specs = [
        pl.BlockSpec((1, blk * ROWS, LANES), lambda s: (2, s, 0)),
        pl.BlockSpec((1, blk * ROWS, LANES), lambda s: (2, s, 1)),
    ]
    to_north, to_south = pl.pallas_call(
        flux_kernel,
        grid=grid,
        in_specs=wind_specs + [bath_spec],
        out_specs=[row, row],
        out_shape=[f32(members, COLS)] * 2,
        compiler_params=clip(24),
        name="flux",
    )(flat, flat, bathymetry)
    fy_n = lax.ppermute(to_south, "lat", south)
    fy_s = lax.ppermute(to_north, "lat", north)

    msg_n, msg_s, wide_bath = pl.pallas_call(
        functools.partial(border_kernel, ROWS),
        grid=grid,
        in_specs=state_specs + [bath_spec, thin, thin, smem],
        out_specs=[whole((MSG, COLS))] * 2 + [whole(wide_bath_shape)],
        out_shape=[f32(MSG, COLS)] * 2 + [f32(*wide_bath_shape)],
        compiler_params=clip(24),
        name="border",
    )(flat, flat, bathymetry, from_east, from_west, fcor)
    got_n = lax.ppermute(msg_s, "lat", south)
    got_s = lax.ppermute(msg_n, "lat", north)

    one = lambda x: x.reshape(1, slots)
    obs = whole((1, slots))
    edge = whole((2, members, WIDE))
    wb_spec, bey_spec = whole(wide_bath_shape), whole((4, CH, WIDE))
    fields_shape = VM((3, ROWS, members, COLS), jnp.float32)
    fields, flux_edge, height_edge, wind_edge, seen, late_n, late_s = pl.pallas_call(
        functools.partial(local_kernel, ROWS),
        grid=grid,
        in_specs=state_specs + [wb_spec, thin, thin, smem, obs],
        out_specs=[
            pl.BlockSpec((3, ROWS, blk, COLS), lambda s: (0, 0, s, 0)),
            pl.BlockSpec((2, blk, WIDE), lambda s: (0, s, 0)),
            pl.BlockSpec((2, blk, WIDE), lambda s: (0, s, 0)),
            pl.BlockSpec((2, blk, COLS), lambda s: (0, s, 0)),
            whole((members, slots)),
            row,
            row,
        ],
        out_shape=[
            fields_shape, f32(2, members, WIDE), f32(2, members, WIDE),
            f32(2, members, COLS), f32(members, slots), f32(members, COLS), f32(members, COLS),
        ],
        scratch_shapes=[VM((ROWS, members, COLS), jnp.float32)],
        compiler_params=clip(24),
        name="local",
    )(flat, flat, wide_bath, from_east, from_west, fcor, one(obs_index))

    part = f32(136, LANES)
    mine, theirs, beyond = pl.pallas_call(
        functools.partial(sums_kernel, nlat, members, math.sqrt(slots * nlat * nlon) / 16.0),
        grid=(1,),
        in_specs=[wb_spec]
        + [whole((members, COLS))] * 2
        + [whole((MSG, COLS))] * 2
        + [edge, edge, whole((members, slots)), obs, smem, obs, obs],
        out_specs=[whole(part.shape), whole(part.shape), bey_spec],
        out_shape=[part, part, f32(4, CH, WIDE)],
        scratch_shapes=[VM((6, members, COLS), jnp.float32), VM((272, LANES), jnp.float32)],
        compiler_params=clip(24),
        name="sums",
    )(
        wide_bath, fy_n, fy_s, got_n, got_s, flux_edge, height_edge, seen,
        one(obs_index), obs_count, one(obs_value), one(obs_sd),
    )

    pieces = [(64, 64), (32, 32), (16, 16), (128, 128), (0, 8), (8, 8)]
    for lead, size in pieces:
        at = lambda rows, j: pl.BlockSpec((rows, COLS), lambda s: (j, 0))
        msg_specs = [at(size, lead // size), at(size, (COLS + lead) // size), at(CH, EXT // CH + lead // (2 * blk))]
        edge_k = pl.BlockSpec((2, size, WIDE), lambda s, j=lead // size: (0, j, 0))
        wind_k = pl.BlockSpec((2, size, COLS), lambda s, j=lead // size: (0, j, 0))
        here = pl.BlockSpec(memory_space=VM)
        fields = pl.pallas_call(
            functools.partial(complete_kernel, ROWS, nlat, lead),
            grid=(1,),
            in_specs=[wb_spec, bey_spec, smem, at(size, lead // size), at(size, lead // size)]
            + msg_specs * 2
            + [edge_k, edge_k, wind_k, here],
            out_specs=here,
            out_shape=fields_shape,
            input_output_aliases={14: 0},
            compiler_params=clip(24),
            name="complete",
        )(
            wide_bath, beyond, fcor, fy_n, fy_s, got_n, got_n, got_n, got_s, got_s, got_s,
            flux_edge, height_edge, wind_edge, fields,
        )

    sum_mine, sum_other, late = total(mine, theirs, late_n, late_s, south, north)
    fields = pltpu.with_memory_space_constraint(fields, pltpu.VMEM)

    mix = pl.pallas_call(
        functools.partial(factor_kernel, members),
        out_shape=f32(members, members),
        in_specs=[pl.BlockSpec(memory_space=VM)] * 2,
        out_specs=pl.BlockSpec(memory_space=VM),
        scratch_shapes=[VM((members, LANES), jnp.float32), VM((272, LANES), jnp.float32)],
        compiler_params=clip(8),
        name="factor",
    )(sum_mine, sum_other)

    half = pl.BlockSpec((members, LANES), lambda c, j: (0, j))
    analysis = pl.pallas_call(
        apply_kernel,
        grid=(3, COLS // LANES),
        in_specs=[
            whole((members, members)),
            pl.BlockSpec((1, ROWS, members, LANES), lambda c, j: (c, 0, 0, j)),
            half,
            half,
        ],
        out_specs=pl.BlockSpec((1, members * ROWS, LANES), lambda c, j: (c, 0, j)),
        out_shape=f32(3, members * ROWS, COLS),
        scratch_shapes=[VM((members, 3 * members), jnp.bfloat16)],
        compiler_params=clip(24),
        name="mix",
    )(mix, fields, *late)
    return analysis.reshape(state.shape)


def solution(mesh):
    return jax.shard_map(
        body,
        mesh=mesh,
        in_specs=(
            P(None, None, "lat", "lon"),
            P("lat", "lon"),
            P("lat", "lon", None),
            P("lat", "lon"),
            P("lat", "lon", None),
            P("lat", "lon", None),
        ),
        out_specs=P(None, None, "lat", "lon"),
        check_vma=False,
    )
```

```python
import functools
import math

import jax
import jax.numpy as jnp
import numpy as np
from jax import lax
from jax.experimental import pallas as pl
from jax.experimental.pallas import tpu as pltpu
from jax.sharding import PartitionSpec as P


HI = lax.Precision.HIGHEST
CH = 8
PER = 8
ROWS = 8
COLS = 256
WIDE = 384
LANES = 128
EXT = 2 * COLS
BATH = EXT + 16
MSG = BATH + 8
VM = pltpu.VMEM


def each(trips, fn, together):
    def turn(t, carry):
        for j in range(together):
            carry = fn(t * together + j, carry)
        return carry

    return lambda init: lax.fori_loop(0, trips // together, turn, init)


def roll(x, shift):
    return pltpu.roll(x, shift % x.shape[1], 1)


def ddx(x):
    return roll(x, -1) - roll(x, 1)


def ext_at(block, row):
    half = pl.ds(pl.multiple_of((block % 2) * LANES, LANES), LANES)
    return pl.ds(pl.multiple_of(row + (block // 2) * CH, CH), CH), half


def lanes_of(shape):
    return lax.broadcasted_iota(jnp.int32, shape, 1)


def field_rows(lo, hi, c, q, i):
    rows = pl.ds(q * (CH * ROWS) + i, CH, stride=ROWS)
    return lo[c, rows, :], hi[c, rows, :]


def flux_kernel(lo, hi, bath, to_north, to_south):
    def chunk(q, carry):
        out = pl.ds(pl.multiple_of(q * CH, CH), CH)
        for i, ref in ((0, to_north), (ROWS - 1, to_south)):
            a, b = field_rows(lo, hi, 0, q, i)
            ref[out, :LANES] = a * bath[i : i + 1, :LANES]
            ref[out, LANES:] = b * bath[i : i + 1, LANES:]
        return carry

    each(PER, chunk, 4)(0)


def edges_kernel(lo, hi, bath, to_east, to_west):
    lane = lanes_of((CH, LANES))
    first = jnp.zeros((CH, LANES), jnp.float32)
    last = jnp.zeros((CH, LANES), jnp.float32)
    place = lambda spot: (lane >= spot) & (lane < spot + 4)
    for i in range(ROWS):
        spot = 4 * (3 * ROWS + i)
        a = jnp.broadcast_to(bath[i : i + 1, :LANES], (CH, LANES))
        b = jnp.broadcast_to(bath[i : i + 1, LANES:], (CH, LANES))
        first = jnp.where(place(spot), roll(a, spot), first)
        last = jnp.where(place(spot), roll(b, spot + 4), last)

    def chunk(q, carry):
        west, east = first, last
        out = pl.ds(pl.multiple_of(q * CH, CH), CH)
        for c in range(3):
            for i in range(ROWS):
                a, b = field_rows(lo, hi, c, q, i)
                spot = 4 * (c * ROWS + i)
                west = jnp.where(place(spot), roll(a, spot), west)
                east = jnp.where(place(spot), roll(b, spot + 4), east)
        to_east[out, :] = east
        to_west[out, :] = west
        return carry

    each(PER, chunk, 2)(0)


def bath_rows(bath, from_east, from_west, wide_bath):
    lane = lanes_of((CH, LANES))
    e, w = from_east[0:CH, :], from_west[0:CH, :]
    for i in range(ROWS):
        spot = 4 * (3 * ROWS + i)
        tail = jnp.where(lane < 4, roll(e, -spot), roll(w, 124 - spot))
        wide_bath[i, :, :COLS] = jnp.broadcast_to(bath[i : i + 1, :], (CH, COLS))
        wide_bath[i, :, COLS:] = tail


def wide_rows(lo, hi, e, w, lane, q, c, i):
    a, b = field_rows(lo, hi, c, q, i)
    spot = 4 * (c * ROWS + i)
    tail = jnp.where(lane < 4, roll(e, -spot), roll(w, 124 - spot))
    return jnp.concatenate([a, b, tail], axis=1)


def border_kernel(nrows, lo, hi, bath, from_east, from_west, fcor, msg_n, msg_s, wide_bath):
    step = pl.program_id(0)
    base = lax.axis_index("lat") * nrows

    @pl.when(step == 0)
    def _():
        bath_rows(bath, from_east, from_west, wide_bath)
        for msg, r0, r1 in ((msg_n, 0, 1), (msg_s, ROWS - 1, ROWS - 2)):
            msg[EXT:MSG, :] = jnp.zeros((MSG - EXT, COLS), jnp.float32)
            msg[BATH : BATH + 1, :] = bath[r0 : r0 + 1, :]
            msg[BATH + 1 : BATH + 2, :] = bath[r1 : r1 + 1, :]
            msg[BATH + 2 : BATH + 3, :LANES] = wide_bath[r0, 0:1, COLS:]

    lane = lanes_of((CH, LANES))

    def chunk(q, carry):
        out = pl.ds(pl.multiple_of(q * CH, CH), CH)
        dst = pl.ds(pl.multiple_of(step * (CH * PER) + q * CH, CH), CH)
        dst_q = pl.ds(pl.multiple_of(COLS + step * (CH * PER) + q * CH, CH), CH)
        e, w = from_east[out, :], from_west[out, :]
        new = []
        for msg, first, sg, ext in ((msg_n, 0, 1, carry[0]), (msg_s, ROWS - 1, -1, carry[1])):
            rows = [first + sg * k for k in range(3)]
            H = [wide_bath[r] for r in rows]
            load = lambda c, k: wide_rows(lo, hi, e, w, lane, q, c, rows[k])
            h = [load(0, k) for k in range(2)]
            u = [load(1, k) for k in range(2)]
            v = [load(2, k) for k in range(3)]
            f0 = fcor[base + rows[0]]
            fy = [H[k] * v[k] for k in range(3)]
            dfx = [ddx(H[k] * u[k]) for k in range(2)]
            h1a = h[1] - 0.25 * (dfx[1] + sg * (fy[2] - fy[0]))
            part = h[0] - 0.25 * (dfx[0] + sg * fy[1])
            flux = H[0] * (v[0] - (0.5 * f0) * u[0] - (sg * 0.25) * h1a)
            msg[dst, :] = part[:, :COLS]
            msg[dst_q, :] = flux[:, :COLS]
            t = jnp.where(
                lane < 8,
                roll(fy[0][:, COLS:], 4),
                jnp.where(lane < 12, roll(part[:, COLS:], 10), roll(flux[:, COLS:], 14)),
            )
            t = pltpu.roll(t, q * 16, 1)
            new.append(jnp.where(lane // 16 == q, t, ext))
        return tuple(new)

    zero = jnp.zeros((CH, LANES), jnp.float32)
    exts = each(PER, chunk, 4)((zero, zero))
    for msg, ext in ((msg_n, exts[0]), (msg_s, exts[1])):
        msg[ext_at(step, EXT)] = ext


def split(x, pieces):
    parts = []
    for k in range(pieces):
        p = x.astype(jnp.bfloat16)
        parts.append(p)
        if k + 1 < pieces:
            x = x - p.astype(jnp.float32)
    return parts


def dot(a, b, ca, cb):
    return lax.dot_general(
        a, b, (((ca,), (cb,)), ((), ())), precision=HI, preferred_element_type=jnp.float32
    )


def bdot(a, b):
    return jnp.dot(a, b, preferred_element_type=jnp.float32)


def clip(limit):
    return pltpu.CompilerParams(vmem_limit_bytes=limit << 20)


def local_kernel(
    nrows, lo, hi, wide_bath, from_east, from_west, fcor, index,
    out, flux_edge, height_edge, wind_edge, seen, late_n, late_s, height,
):
    step = pl.program_id(0)
    base = lax.axis_index("lat") * nrows
    lane = lanes_of((CH, LANES))

    def across(y, i):
        if i == 0:
            return y[1]
        if i == ROWS - 1:
            return -y[i - 1]
        return y[i + 1] - y[i - 1]

    def chunk(q, carry):
        loc = pl.ds(pl.multiple_of(q * CH, CH), CH)
        dst = pl.ds(pl.multiple_of(step * (CH * PER) + q * CH, CH), CH)
        e, w = from_east[loc, :], from_west[loc, :]
        load = lambda c, i: wide_rows(lo, hi, e, w, lane, q, c, i)
        H = [wide_bath[i] for i in range(ROWS)]
        f = [fcor[base + i] for i in range(ROWS)]
        h = [load(0, i) for i in range(ROWS)]
        u = [load(1, i) for i in range(ROWS)]
        v = [load(2, i) for i in range(ROWS)]
        fy = [H[i] * v[i] for i in range(ROWS)]
        h1 = [h[i] - 0.25 * (ddx(H[i] * u[i]) + across(fy, i)) for i in range(ROWS)]
        u1 = [u[i] + (0.5 * f[i]) * v[i] - 0.25 * ddx(h1[i]) for i in range(ROWS)]
        v1 = [v[i] - (0.5 * f[i]) * u[i] - 0.25 * across(h1, i) for i in range(ROWS)]
        for k, i in ((0, 0), (1, ROWS - 1)):
            flux_edge[k, loc, :] = fy[i]
            height_edge[k, loc, :] = h1[i]
            wind_edge[k, loc, :] = v1[i][:, :COLS]
        fy = [H[i] * v1[i] for i in range(ROWS)]
        h2 = [h1[i] - 0.25 * (ddx(H[i] * u1[i]) + across(fy, i)) for i in range(ROWS)]
        for i in range(ROWS):
            u2 = u1[i] + (0.5 * f[i]) * v1[i] - 0.25 * ddx(h2[i])
            v2 = v1[i] - (0.5 * f[i]) * u1[i] - 0.25 * across(h2, i)
            out[0, i, loc, :] = h2[i][:, :COLS]
            out[1, i, loc, :] = u2[:, :COLS]
            out[2, i, loc, :] = v2[:, :COLS]
            height[i, dst, :] = h2[i][:, :COLS]
        late_n[loc, :] = h2[0][:, :COLS]
        late_s[loc, :] = h2[-1][:, :COLS]
        return carry

    lax.fori_loop(0, PER, chunk, 0)

    @pl.when(step == pl.num_programs(0) - 1)
    def _():
        seen[...] = observe(index, [(i, height[i]) for i in range(ROWS)], 3)


def observe(index, planes, count):
    slots = index.shape[1]
    sub = lax.broadcasted_iota(jnp.int32, (COLS, slots), 0)
    cell = jnp.broadcast_to(index[...], (COLS, slots))
    left, right = [], []
    for i, plane in planes:
        pick = jnp.where(sub + i * COLS == cell, 1.0, 0.0).astype(jnp.bfloat16)
        left += split(plane, count)
        right += [pick] * count
    return bdot(jnp.concatenate(left, axis=1), jnp.concatenate(right, axis=0))


def beyond_rows(msgs, beyond):
    for k, msg in enumerate(msgs):
        beyond[2 * k, :, :COLS] = jnp.broadcast_to(msg[BATH : BATH + 1, :], (CH, COLS))
        beyond[2 * k, :, COLS:] = jnp.broadcast_to(msg[BATH + 2 : BATH + 3, :LANES], (CH, LANES))
        beyond[2 * k + 1, :, :COLS] = jnp.broadcast_to(msg[BATH + 1 : BATH + 2, :], (CH, COLS))
        beyond[2 * k + 1, :, COLS:] = jnp.zeros((CH, LANES), jnp.float32)


def edge_change(k, has, q, chunk, fy_row, part_row, flux_row, ext, flux_edge, height_edge, wide_bath, beyond):
    sg, e, n = ((-1, 0, 1), (1, ROWS - 1, ROWS - 2))[k]
    rows = pl.ds(pl.multiple_of(q * CH, CH), CH)
    t = pltpu.roll(ext, (LANES - chunk * 16) % LANES, 1)
    g0 = jnp.concatenate([fy_row, roll(t, -4)], axis=1)
    part = jnp.concatenate([part_row, roll(t, -10)], axis=1)
    flux = jnp.concatenate([flux_row, roll(t, -14)], axis=1)
    c = sg * 0.25
    eps = c * flux_edge[k, rows, :]
    dh1 = -c * g0
    du1 = -0.25 * ddx(dh1)
    dv_e = -c * (has * (part + eps))
    dv_n = -c * dh1
    h1 = height_edge[k, rows, :] + dh1
    g2 = flux + c * (beyond[2 * k] * h1)
    He, Hn = wide_bath[e], wide_bath[n]
    flow_n = Hn * dv_n
    a = dh1 - 0.25 * (ddx(He * du1) - sg * flow_n + sg * g2)
    b = -c * (He * dv_e)
    d = -c * flow_n
    return eps, du1, dv_e, dv_n, a, b, d


def sums_kernel(
    ntiles, members, scale,
    wide_bath, fy_n, fy_s, msg_n, msg_s, flux_edge, height_edge, seen, index, count, value, sd,
    mine, theirs, beyond, change, sums,
):
    tile = lax.axis_index("lat")
    has = (jnp.where(tile > 0, 1.0, 0.0), jnp.where(tile < ntiles - 1, 1.0, 0.0))
    beyond_rows((msg_n, msg_s), beyond)
    slots = index.shape[1]

    def chunk(q, carry):
        dst = pl.ds(pl.multiple_of(q * CH, CH), CH)
        for k, fy, msg in ((0, fy_n, msg_n), (1, fy_s, msg_s)):
            far = pl.ds(pl.multiple_of(COLS + q * CH, CH), CH)
            ext = msg[ext_at(q // PER, EXT)]
            new = edge_change(
                k, has[k], q, q % PER, fy[dst, :], msg[dst, :], msg[far, :], ext,
                flux_edge, height_edge, wide_bath, beyond,
            )
            for j in range(3):
                change[3 * k + j, dst, :] = new[4 + j][:, :COLS]
        return carry

    each(members // CH, chunk, 4)(0)
    rows = (0, 1, 2, ROWS - 1, ROWS - 2, ROWS - 3)
    hx = seen[...] + observe(index, [(r, change[j]) for j, r in enumerate(rows)], 2)
    used = jnp.where(lanes_of((1, slots)) < count[0, 0], 1.0, 0.0)
    sigma = sd[...] * scale
    hmean = jnp.mean(hx, axis=0, keepdims=True)
    anom = (hx - hmean) * (used / (math.sqrt(members - 1) * sigma))
    innov = (value[...] - hmean) / sigma * used
    gram = dot(anom, anom, 1, 1)
    proj = dot(jnp.broadcast_to(innov, (8, slots)), anom, 1, 1)
    n = LANES
    ln, sb = lanes_of((n, n)), lax.broadcasted_iota(jnp.int32, (n, n), 0)
    last = gram[n:, n:]
    sums[0:n, :] = jnp.where(ln >= sb, gram[:n, :n], last)
    sums[n : 2 * n, :] = gram[:n, n:]
    sums[2 * n :, :] = jnp.zeros((16, n), jnp.float32)
    sums[2 * n : 2 * n + 1, :] = jnp.sum(jnp.where(ln == sb, last, 0.0), axis=0, keepdims=True)
    sums[2 * n + 1 : 2 * n + 2, :] = proj[0:1, :n]
    sums[2 * n + 2 : 2 * n + 3, :] = proj[0:1, n:]
    part = mine.shape[0]
    core = lax.axis_index("lon") % 2
    mine[...] = sums[pl.ds(pl.multiple_of(core * part, 8), part), :]
    theirs[...] = sums[pl.ds(pl.multiple_of((1 - core) * part, 8), part), :]


def complete_kernel(
    nrows, ntiles, first, wide_bath, beyond, fcor, fy_n, fy_s,
    part_n, flux_n, ext_n, part_s, flux_s, ext_s, flux_edge, height_edge, wind_edge, fields, out,
):
    tile = lax.axis_index("lat")
    base = tile * nrows
    has = (jnp.where(tile > 0, 1.0, 0.0), jnp.where(tile < ntiles - 1, 1.0, 0.0))

    def chunk(q, carry):
        loc = pl.ds(pl.multiple_of(q * CH, CH), CH)
        rows = loc
        full = first // CH + q
        there = pl.ds(pl.multiple_of(first + q * CH, CH), CH)
        for k, sg, e, fy, part, flux, ext in (
            (0, -1, 0, fy_n, part_n, flux_n, ext_n),
            (1, 1, ROWS - 1, fy_s, part_s, flux_s, ext_s),
        ):
            eps, du1, dv_e, dv_n, a, b, d = edge_change(
                k, has[k], q, full % PER, fy[loc, :], part[loc, :], flux[loc, :], ext[ext_at((full // PER) % 2, 0)],
                flux_edge, height_edge, wide_bath, beyond,
            )
            c = sg * 0.25
            flow = wide_bath[e] * dv_e
            flow = flow[:, :COLS] + wide_bath[e][:, :COLS] * wind_edge[k, rows, :]
            bend = ddx(beyond[2 * k] * (-0.25 * ddx(eps))) + 0.25 * (beyond[2 * k + 1] * eps)
            g3 = has[k] * (eps[:, :COLS] - 0.25 * (bend[:, :COLS] - sg * flow))
            cut = lambda x: x[:, :COLS]
            f0, f1 = 0.5 * fcor[base + e], 0.5 * fcor[base + e - sg]
            r = [e - sg * j for j in range(4)]
            upd = (
                (0, r[0], cut(a)),
                (0, r[1], cut(b)),
                (0, r[2], cut(d)),
                (1, r[0], cut(du1 + f0 * dv_e - 0.25 * ddx(a))),
                (1, r[1], cut(f1 * dv_n - 0.25 * ddx(b))),
                (1, r[2], cut(-0.25 * ddx(d))),
                (2, r[0], cut(dv_e - f0 * du1) - c * (g3 - cut(b))),
                (2, r[1], cut(dv_n - c * (a - d))),
                (2, r[2], cut(-c * b)),
                (2, r[3], cut(-c * d)),
            )
            for i, j, x in upd:
                out[i, j, there, :] = fields[i, j, there, :] + x
        return carry

    trips = fy_n.shape[0] // CH
    each(trips, chunk, min(4, trips))(0)


def elim(a, dst, base):
    n = LANES
    groups = n // 8
    lane = lanes_of((8, n))
    sub = lax.broadcasted_iota(jnp.int32, (8, n), 0)
    A = [a[8 * g : 8 * g + 8, :] for g in range(groups)]
    X = [(lane == sub + 8 * g).astype(jnp.float32) for g in range(groups)]

    def body(live, it, carry):
        A, X = list(carry[:live]), list(carry[live:])
        column = lambda g, k: jnp.broadcast_to(A[g][:, k : k + 1], (8, n))
        C, P, Z = [column(0, k) for k in range(8)], A[0], X[0]
        rows = Z
        for k in range(8):
            pick = lambda x: jnp.broadcast_to(x[k : k + 1, :], (8, n))
            here = sub == k
            d = pick(C[k])
            inv = 1.0 / d
            rows = jnp.where(here, Z * lax.rsqrt(d), rows)
            ra, rx = pick(P) * inv, pick(Z) * inv
            for j in range(k + 1, 8):
                rc = pick(C[j]) * inv
                C[j] = jnp.where(here, rc, C[j] - C[k] * rc)
            P = jnp.where(here, ra, P - C[k] * ra)
            Z = jnp.where(here, rx, Z - C[k] * rx)
        dst[pl.ds(pl.multiple_of(base + it * 8, 8), 8), :] = rows
        spread = lambda x: [jnp.broadcast_to(x[k : k + 1, :], (8, n)) for k in range(8)]
        rp, rz = spread(P), spread(Z)
        for g in range(1, live):
            cols = [column(g, k) for k in range(8)]
            for k in range(8):
                A[g] = A[g] - cols[k] * rp[k]
                X[g] = X[g] - cols[k] * rz[k]
        z = jnp.zeros((8, n), jnp.float32)
        A = [roll(A[g], -8) for g in range(1, live)] + [z]
        return tuple(A) + tuple(X[1:]) + (z,)

    seg = 2
    for first in range(0, groups, seg):
        live = groups - first
        out = lax.fori_loop(first, first + seg, functools.partial(body, live), tuple(A) + tuple(X))
        A, X = list(out[: live - seg]), list(out[live : 2 * live - seg])


def factor_kernel(members, mine, other, mix, inverse, g_ref):
    n = LANES
    part = mine.shape[0]
    core = lax.axis_index("lon") % 2
    g_ref[pl.ds(pl.multiple_of(core * part, 8), part), :] = mine[...]
    g_ref[pl.ds(pl.multiple_of((1 - core) * part, 8), part), :] = other[...]
    lane, sub = lanes_of((n, n)), lax.broadcasted_iota(jnp.int32, (n, n), 0)
    both = g_ref[0:n, :]
    g12 = g_ref[n : 2 * n, :]
    tail = g_ref[2 * n : 2 * n + 8, :]
    eye = (lane == sub).astype(jnp.float32)
    up = jnp.where(lane >= sub, both, 0.0)
    low = jnp.where(lane < sub, both, 0.0)
    g11 = up + jnp.where(lane > sub, up, 0.0).T + eye
    g22 = low + low.T + jnp.where(lane == sub, jnp.broadcast_to(tail[0:1, :], (n, n)), 0.0) + eye
    elim(g11, inverse, 0)
    x11 = inverse[0:n, :]
    y12 = dot(x11, g12, 1, 0)
    elim(g22 - dot(y12, y12, 0, 0), inverse, n)
    x22 = inverse[n : 2 * n, :]
    x21 = -dot(x22, dot(y12, x11, 0, 0), 1, 0)
    p1 = jnp.broadcast_to(tail[1:2, :], (8, n))
    p2 = jnp.broadcast_to(tail[2:3, :], (8, n))
    q1 = dot(p1, x11, 1, 1)
    q2 = dot(p1, x21, 1, 1) + dot(p2, x22, 1, 1)
    c = 1.0 / math.sqrt(members - 1)
    w1 = (dot(q1, x11, 1, 0) + dot(q2, x21, 1, 0))[0:1, :] * c
    w2 = dot(q2, x22, 1, 0)[0:1, :] * c
    ws = jnp.sum(w1, axis=1, keepdims=True) + jnp.sum(w2, axis=1, keepdims=True)
    r = 1.0 / members
    s1 = (1.0 - ws - jnp.sum(x11, axis=1, keepdims=True)) * r
    s2 = (1.0 - ws - jnp.sum(x21, axis=1, keepdims=True) - jnp.sum(x22, axis=1, keepdims=True)) * r
    mix[0:n, 0:n] = x11 + (w1 + s1)
    mix[0:n, n:] = w2 + s1
    mix[n:, 0:n] = x21 + (w1 + s2)
    mix[n:, n:] = x22 + (w2 + s2)


def apply_kernel(mix, fields, late_n, late_s, out, left):
    members = mix.shape[0]

    @pl.when((pl.program_id(0) == 0) & (pl.program_id(1) == 0))
    def _():
        high, low = split(mix[...], 2)
        left[:, :members] = high
        left[:, members : 2 * members] = high
        left[:, 2 * members :] = low

    wind = jnp.where(pl.program_id(0) == 2, 0.25, 0.0)
    lanes = pl.ds(pl.multiple_of(pl.program_id(1) * LANES, LANES), LANES)
    for i in range(ROWS):
        x = fields[pl.program_id(0), i, :, lanes]
        if i == 0:
            x = x + wind * late_n[...]
        if i == ROWS - 1:
            x = x - wind * late_s[...]
        a, b = split(x, 2)
        out[0, pl.ds(i, members, stride=ROWS), :] = bdot(left[...], jnp.concatenate([a, b, a], axis=0))


def whole(shape):
    return pl.BlockSpec(shape, lambda *_: (0,) * len(shape))


def f32(*shape):
    return jax.ShapeDtypeStruct(shape, jnp.float32)


def flips(n, bit):
    return [(i, i ^ bit) for i in range(n)]


def bits(n):
    return [1 << k for k in range(n.bit_length() - 1)]


def total(mine, theirs, late_n, late_s, south, north):
    nlon, nlat = lax.axis_size("lon"), lax.axis_size("lat")
    y = mine + lax.ppermute(theirs, "lon", flips(nlon, 1))
    lon, lat = bits(nlon), bits(nlat)
    stages = [("lat", nlat, lat[:1]), ("lon", nlon, lon[1:3]), ("lon", nlon, lon[3:]), ("lat", nlat, lat[1:])]
    late = []
    for k, (axis, n, todo) in enumerate(stages):
        hops = todo if len(todo) == 1 else [todo[0], todo[1], todo[0] | todo[1]]
        if k == 2:
            y, late_s = lax.optimization_barrier((y, late_s))
            late.append(lax.ppermute(late_s, "lat", south))
        if k == 3:
            y, late_n = lax.optimization_barrier((y, late_n))
            late.append(lax.ppermute(late_n, "lat", north))
        parts = [lax.ppermute(y, axis, flips(n, b)) for b in hops]
        for p in parts:
            y = y + p
    other = lax.ppermute(y, "lon", flips(nlon, 1))
    return y, other, late


def body(state, bathymetry, obs_index, obs_count, obs_value, obs_sd):
    members = state.shape[1]
    nlat, nlon = lax.axis_size("lat"), lax.axis_size("lon")
    slots = obs_index.shape[2]
    total_rows = ROWS * nlat
    fcor = np.sin(math.pi / 3.0 * ((np.arange(total_rows) + 0.5) / total_rows - 0.5)).astype(np.float32)
    flat = pltpu.with_memory_space_constraint(state.reshape(3, members * ROWS, COLS), pltpu.HBM)
    blk = CH * PER
    grid = (members // blk,)
    state_specs = [
        pl.BlockSpec((3, blk * ROWS, LANES), lambda s: (0, s, 0)),
        pl.BlockSpec((3, blk * ROWS, LANES), lambda s: (0, s, 1)),
    ]
    thin = pl.BlockSpec((blk, LANES), lambda s: (s, 0))
    row = pl.BlockSpec((blk, COLS), lambda s: (s, 0))
    bath_spec = whole((ROWS, COLS))
    smem = pl.BlockSpec(memory_space=pltpu.SMEM)

    wide_bath_shape = (ROWS, CH, WIDE)
    east = [(i, (i + 1) % nlon) for i in range(nlon)]
    west = [(j, i) for i, j in east]
    south = [(i, i + 1) for i in range(nlat - 1)]
    north = [(j, i) for i, j in south]

    to_east, to_west = pl.pallas_call(
        edges_kernel,
        grid=grid,
        in_specs=state_specs + [bath_spec],
        out_specs=[thin, thin],
        out_shape=[f32(members, LANES)] * 2,
        compiler_params=clip(24),
        name="edges",
    )(flat, flat, bathymetry)
    from_west = lax.ppermute(to_east, "lon", east)
    from_east = lax.ppermute(to_west, "lon", west)

    wind_specs = [
        pl.BlockSpec((1, blk * ROWS, LANES), lambda s: (2, s, 0)),
        pl.BlockSpec((1, blk * ROWS, LANES), lambda s: (2, s, 1)),
    ]
    to_north, to_south = pl.pallas_call(
        flux_kernel,
        grid=grid,
        in_specs=wind_specs + [bath_spec],
        out_specs=[row, row],
        out_shape=[f32(members, COLS)] * 2,
        compiler_params=clip(24),
        name="flux",
    )(flat, flat, bathymetry)
    fy_n = lax.ppermute(to_south, "lat", south)
    fy_s = lax.ppermute(to_north, "lat", north)

    msg_n, msg_s, wide_bath = pl.pallas_call(
        functools.partial(border_kernel, ROWS),
        grid=grid,
        in_specs=state_specs + [bath_spec, thin, thin, smem],
        out_specs=[whole((MSG, COLS))] * 2 + [whole(wide_bath_shape)],
        out_shape=[f32(MSG, COLS)] * 2 + [f32(*wide_bath_shape)],
        compiler_params=clip(24),
        name="border",
    )(flat, flat, bathymetry, from_east, from_west, fcor)
    got_n = lax.ppermute(msg_s, "lat", south)
    got_s = lax.ppermute(msg_n, "lat", north)

    one = lambda x: x.reshape(1, slots)
    obs = whole((1, slots))
    edge = whole((2, members, WIDE))
    wb_spec, bey_spec = whole(wide_bath_shape), whole((4, CH, WIDE))
    fields_shape = VM((3, ROWS, members, COLS), jnp.float32)
    fields, flux_edge, height_edge, wind_edge, seen, late_n, late_s = pl.pallas_call(
        functools.partial(local_kernel, ROWS),
        grid=grid,
        in_specs=state_specs + [wb_spec, thin, thin, smem, obs],
        out_specs=[
            pl.BlockSpec((3, ROWS, blk, COLS), lambda s: (0, 0, s, 0)),
            pl.BlockSpec((2, blk, WIDE), lambda s: (0, s, 0)),
            pl.BlockSpec((2, blk, WIDE), lambda s: (0, s, 0)),
            pl.BlockSpec((2, blk, COLS), lambda s: (0, s, 0)),
            whole((members, slots)),
            row,
            row,
        ],
        out_shape=[
            fields_shape, f32(2, members, WIDE), f32(2, members, WIDE),
            f32(2, members, COLS), f32(members, slots), f32(members, COLS), f32(members, COLS),
        ],
        scratch_shapes=[VM((ROWS, members, COLS), jnp.float32)],
        compiler_params=clip(24),
        name="local",
    )(flat, flat, wide_bath, from_east, from_west, fcor, one(obs_index))

    part = f32(136, LANES)
    mine, theirs, beyond = pl.pallas_call(
        functools.partial(sums_kernel, nlat, members, math.sqrt(slots * nlat * nlon) / 16.0),
        grid=(1,),
        in_specs=[wb_spec]
        + [whole((members, COLS))] * 2
        + [whole((MSG, COLS))] * 2
        + [edge, edge, whole((members, slots)), obs, smem, obs, obs],
        out_specs=[whole(part.shape), whole(part.shape), bey_spec],
        out_shape=[part, part, f32(4, CH, WIDE)],
        scratch_shapes=[VM((6, members, COLS), jnp.float32), VM((272, LANES), jnp.float32)],
        compiler_params=clip(24),
        name="sums",
    )(
        wide_bath, fy_n, fy_s, got_n, got_s, flux_edge, height_edge, seen,
        one(obs_index), obs_count, one(obs_value), one(obs_sd),
    )

    pieces = [(64, 64), (32, 32), (16, 16), (128, 128), (0, 8), (8, 8)]
    for lead, size in pieces:
        at = lambda rows, j: pl.BlockSpec((rows, COLS), lambda s: (j, 0))
        msg_specs = [at(size, lead // size), at(size, (COLS + lead) // size), at(CH, EXT // CH + lead // (2 * blk))]
        edge_k = pl.BlockSpec((2, size, WIDE), lambda s, j=lead // size: (0, j, 0))
        wind_k = pl.BlockSpec((2, size, COLS), lambda s, j=lead // size: (0, j, 0))
        here = pl.BlockSpec(memory_space=VM)
        fields = pl.pallas_call(
            functools.partial(complete_kernel, ROWS, nlat, lead),
            grid=(1,),
            in_specs=[wb_spec, bey_spec, smem, at(size, lead // size), at(size, lead // size)]
            + msg_specs * 2
            + [edge_k, edge_k, wind_k, here],
            out_specs=here,
            out_shape=fields_shape,
            input_output_aliases={14: 0},
            compiler_params=clip(24),
            name="complete",
        )(
            wide_bath, beyond, fcor, fy_n, fy_s, got_n, got_n, got_n, got_s, got_s, got_s,
            flux_edge, height_edge, wind_edge, fields,
        )

    sum_mine, sum_other, late = total(mine, theirs, late_n, late_s, south, north)
    fields = pltpu.with_memory_space_constraint(fields, pltpu.VMEM)

    mix = pl.pallas_call(
        functools.partial(factor_kernel, members),
        out_shape=f32(members, members),
        in_specs=[pl.BlockSpec(memory_space=VM)] * 2,
        out_specs=pl.BlockSpec(memory_space=VM),
        scratch_shapes=[VM((members, LANES), jnp.float32), VM((272, LANES), jnp.float32)],
        compiler_params=clip(8),
        name="factor",
    )(sum_mine, sum_other)

    half = pl.BlockSpec((members, LANES), lambda c, j: (0, j))
    analysis = pl.pallas_call(
        apply_kernel,
        grid=(3, COLS // LANES),
        in_specs=[
            whole((members, members)),
            pl.BlockSpec(memory_space=VM),
            half,
            half,
        ],
        out_specs=pl.BlockSpec((1, members * ROWS, LANES), lambda c, j: (c, 0, j)),
        out_shape=f32(3, members * ROWS, COLS),
        scratch_shapes=[VM((members, 3 * members), jnp.bfloat16)],
        compiler_params=clip(24),
        name="mix",
    )(mix, fields, *late)
    return analysis.reshape(state.shape)


def solution(mesh):
    return jax.shard_map(
        body,
        mesh=mesh,
        in_specs=(
            P(None, None, "lat", "lon"),
            P("lat", "lon"),
            P("lat", "lon", None),
            P("lat", "lon"),
            P("lat", "lon", None),
            P("lat", "lon", None),
        ),
        out_specs=P(None, None, "lat", "lon"),
        check_vma=False,
    )
```
